1024 devices in a mesh: ctx: 256 (over z, y, core), head: 4 (over x).
Axes of the slice: x: 4, y: 4, z: 32, core: 2. Of those that a mesh axis runs over, the one named last changes fastest.
Arguments:
- query_raw: bfloat16 [32768, 4096], P('ctx', 'head'), may hold values from -6 to 6
- key_raw: bfloat16 [32768, 512], P('ctx', 'head'), may hold values from -6 to 6
- value_in: bfloat16 [32768, 512], P('ctx', 'head'), may hold values from -6 to 6
- grad_out: bfloat16 [32768, 4096], P('ctx', 'head'), may hold values from -16 to 16
- query_gain: float32 [128], replicated, may hold values from 0.25 to 1.75
- key_gain: float32 [128], replicated, may hold values from 0.25 to 1.75
- loss_table: float32 [16], replicated, may hold values from 0.5 to 8
- loss_bucket: int32 [32768], P('ctx'), may hold values from 0 to 15
- block_docs: int32 [256], P('ctx'), may hold values from 0 to 63, never falling along the last dimension, each value on 1 to 11 neighbouring positions
- query_weight: bfloat16 [4096, 4096], P(None, 'head'), may hold values from -0.09375 to 0.09375
Outputs:
- grad_input: bfloat16 [32768, 4096], P('ctx', 'head')
- grad_key: bfloat16 [32768, 512], P('ctx', 'head')
- grad_value: bfloat16 [32768, 512], P('ctx', 'head')
The draws below stay inside these ranges and needn't reach their ends.
Inputs may be any that keep to these rules, and one draw needn't show every extreme that they name: `block_docs`: document ids never decrease along the sequence; every document covers 1 to 11 consecutive blocks, and some document covers exactly 11.
All inputs are finite; a program needn't handle non-finite values.
Results may differ from the reference program's by a relative error of at most 0.012.
Values may be sent and summed in bfloat16 or wider, within the bound.
A program may use at most 32 MiB of HBM per device.

```python
import math
import jax
import jax.numpy as jnp
import numpy as np
from jax import lax

D = 4096
QH = 32
KVH = 4
HD = 128
TOK_DEV = 128
BLOCK = 128
HOPS = 10
NBUCKET = 16
SEQ = 32768
NBLK = 256
MOST = 11
N_CTX = 256


def plant(values, key, low, high):
    longest = values.shape.index(max(values.shape))
    spots = []
    for shift in (0, 1):
        where = [jax.random.randint(jax.random.fold_in(key, axis), (), 0, length) for axis, length in enumerate(values.shape)]
        where[longest] = (where[longest] + shift) % values.shape[longest]
        spots.append(tuple(where))
    return values.at[spots[0]].set(low).at[spots[1]].set(high)


def steps_of(key, shape, shards, low, high):
    level = 1.0
    for dim, parts in shards:
        steps = jax.random.uniform(jax.random.fold_in(jax.random.fold_in(key, 6), dim), (parts,), jnp.float32, low / len(shards), high / len(shards))
        level = level * jnp.repeat(jnp.exp(steps), shape[dim] // parts).reshape((-1,) + (1,) * (len(shape) - 1 - dim))
    return level


def split_up(number_of, total, reach, slope):
    portions = [(1 << 20) // math.isqrt(standing ** slope) + 1 for standing in range(2, number_of + 1)]
    rest, counts = total - reach - (number_of - 1), [1] * (number_of - 1)
    while rest > 0:
        candidates = [i for i in range(number_of - 1) if counts[i] < reach]
        mass, remaining = sum([portions[i] for i in candidates]), rest
        for i in candidates:
            extra = min(reach - counts[i], max(1, remaining * portions[i] // mass), rest)
            counts[i] = counts[i] + extra
            rest = rest - extra
    return np.array([reach] + counts)


def ragged(key, amount, total, bound, lean):
    if amount == 2:
        one = jax.random.randint(key, (), max(1, total - bound), min(bound, total - 1) + 1)
        return jnp.stack([one, total - one])
    lengths = jnp.asarray(split_up(amount, total, bound, lean), jnp.int32)
    twos = (amount - 1) // 2
    giver, sink = lengths[1:1 + 2 * twos:2], lengths[2:2 + 2 * twos:2]
    room = jnp.minimum(giver - 1, bound - sink)
    passed = jax.random.randint(jax.random.fold_in(key, 1), (twos,), 0, 1 << 20) % (room + 1)
    lengths = lengths.at[1:1 + 2 * twos:2].set(giver - passed).at[2:2 + 2 * twos:2].set(sink + passed)
    return lengths[jax.random.permutation(jax.random.fold_in(key, 2), amount)]


def gaussian(key, extent, width, bound, pieces=(), kind=jnp.bfloat16):
    values = jax.random.normal(key, extent, jnp.float32) * width
    if len(pieces) > 0:
        values = steps_of(key, extent, pieces, -0.22, 0.18) * values
    return jnp.clip(values, min=-bound, max=bound).astype(kind)


def setup_inputs(seed: int = 0) -> dict:
    key_list = jax.random.split(jax.random.key(seed), 11)
    return {
        "query_raw": gaussian(key_list[0], (SEQ, QH * HD), 1.0, 6.0, ((0, 256), (1, 4))),
        "key_raw": gaussian(key_list[1], (SEQ, KVH * HD), 1.0, 6.0, ((0, 256), (1, 4))),
        "value_in": gaussian(key_list[2], (SEQ, KVH * HD), 1.0, 6.0, ((0, 256), (1, 4))),
        "grad_out": gaussian(key_list[3], (SEQ, QH * HD), 4.0, 16.0, ((0, 256), (1, 4))),
        "query_gain": jnp.clip(1.0 + 0.15 * jax.random.normal(key_list[4], (HD,), jnp.float32), 0.25, 1.75),
        "key_gain": jnp.clip(1.0 + 0.15 * jax.random.normal(key_list[5], (HD,), jnp.float32), 0.25, 1.75),
        "loss_table": jnp.clip(jnp.exp(jax.random.uniform(key_list[6], (NBUCKET,), jnp.float32, math.log(0.5), math.log(8.0))), 0.5, 8.0),
        "loss_bucket": plant(jax.random.randint(key_list[7], (SEQ,), 0, NBUCKET), jax.random.fold_in(key_list[7], 1), 0, NBUCKET - 1).astype(jnp.int32),
        "block_docs": jnp.searchsorted(jnp.cumsum(ragged(key_list[8], NBLK // 4, NBLK, MOST, 2)), jnp.arange(NBLK), side="right").astype(jnp.int32),
        "query_weight": gaussian(key_list[9], (D, QH * HD), D ** -0.5, 0.09375, ((1, 4),)),
    }


norm_eps = 1e-06

def rms_apply(values, gain):
    mean_square = lax.optimization_barrier(jnp.mean(values * values, axis=-1, keepdims=True))
    return values * lax.rsqrt(mean_square + norm_eps) * gain

def rms_back(values, gain, cotangent):
    result, pullback = jax.vjp(lambda inner: rms_apply(inner, gain), values)
    return pullback(cotangent)[0]

def round_trip(values):
    return lax.optimization_barrier(values.astype(jnp.bfloat16)).astype(jnp.float32)

def reference(query_raw, key_raw, value_in, grad_out, query_gain, key_gain, loss_table, loss_bucket, block_docs, query_weight):
    group = QH // KVH
    scale = HD ** (-0.5)
    margin = HOPS * TOK_DEV
    span = margin + TOK_DEV
    q_float = query_raw.astype(jnp.float32).reshape(SEQ, KVH, group, HD)
    q_hat = rms_apply(q_float, query_gain).astype(jnp.bfloat16)
    k_float = key_raw.astype(jnp.float32).reshape(SEQ, KVH, HD)
    k_hat = rms_apply(k_float, key_gain).astype(jnp.bfloat16)
    values = value_in.reshape(SEQ, KVH, HD)
    grad_rows = grad_out.reshape(SEQ, KVH, group, HD)
    picks = loss_bucket[:, None] == jnp.arange(NBUCKET, dtype=jnp.int32)[None, :]
    tok_weight = lax.optimization_barrier(jnp.sum(jnp.where(picks, loss_table[None, :], jnp.float32(0.0)), axis=1))
    tok_docs = jnp.broadcast_to(block_docs[:, None], (NBLK, BLOCK)).reshape(SEQ)
    k_pad = jnp.concatenate([jnp.zeros((margin, KVH, HD), jnp.bfloat16), k_hat], axis=0)
    v_pad = jnp.concatenate([jnp.zeros((margin, KVH, HD), jnp.bfloat16), values], axis=0)
    doc_pad = jnp.concatenate([jnp.full((margin,), -1, jnp.int32), tok_docs.astype(jnp.int32)], axis=0)
    zero_pad = jnp.zeros((margin + SEQ, KVH, HD), jnp.float32)

    def one_block(carry, index):
        dk_acc, dv_acc = carry
        start = (index * TOK_DEV).astype(jnp.int32)
        q_blk = lax.dynamic_slice_in_dim(q_hat, start, TOK_DEV, 0).astype(jnp.float32)
        qf_blk = lax.dynamic_slice_in_dim(q_float, start, TOK_DEV, 0)
        g_blk = lax.dynamic_slice_in_dim(grad_rows, start, TOK_DEV, 0).astype(jnp.float32)
        w_blk = lax.dynamic_slice_in_dim(tok_weight, start, TOK_DEV, 0)
        qd_blk = lax.dynamic_slice_in_dim(tok_docs, start, TOK_DEV, 0)
        k_win = lax.dynamic_slice_in_dim(k_pad, start, span, 0).astype(jnp.float32)
        v_win = lax.dynamic_slice_in_dim(v_pad, start, span, 0).astype(jnp.float32)
        d_win = lax.dynamic_slice_in_dim(doc_pad, start, span, 0)
        q_pos = start + jnp.arange(TOK_DEV, dtype=jnp.int32)
        k_pos = start - margin + jnp.arange(span, dtype=jnp.int32)
        allowed = (qd_blk[:, None] == d_win[None, :]) & (k_pos[None, :] <= q_pos[:, None]) & (k_pos[None, :] >= 0)
        scores = jnp.einsum('tkgd,skd->kgts', q_blk, k_win) * scale
        exponent = jnp.where(allowed[None, None], jnp.exp(scores), jnp.float32(0.0))
        total = lax.optimization_barrier(jnp.sum(exponent, axis=-1))
        weighted = jnp.einsum('kgts,skd->tkgd', round_trip(exponent), v_win)
        attn_out = weighted / jnp.transpose(total, (2, 0, 1))[..., None]
        delta = w_blk[:, None, None] * lax.optimization_barrier(jnp.sum(g_blk * attn_out, axis=-1))
        attention = exponent / total[..., None]
        weight_row = w_blk[None, None, :, None]
        value_dots = jnp.einsum('tkgd,skd->kgts', g_blk, v_win)
        score_grad = attention * (weight_row * value_dots - jnp.transpose(delta, (1, 2, 0))[..., None])
        ds_half = round_trip(score_grad)
        pw_half = round_trip(attention * weight_row)
        dv_win = jnp.einsum('kgts,tkgd->skd', pw_half, g_blk)
        dk_win = jnp.einsum('kgts,tkgd->skd', ds_half, q_blk) * scale
        dq_hat = jnp.einsum('kgts,skd->tkgd', ds_half, k_win) * scale
        dq_raw = rms_back(qf_blk, query_gain, dq_hat).astype(jnp.bfloat16).reshape(TOK_DEV, QH * HD)
        dx_blk = jnp.dot(dq_raw, query_weight.T, preferred_element_type=jnp.float32).astype(jnp.bfloat16)
        dk_acc = lax.dynamic_update_slice_in_dim(dk_acc, lax.dynamic_slice_in_dim(dk_acc, start, span, 0) + dk_win, start, 0)
        dv_acc = lax.dynamic_update_slice_in_dim(dv_acc, lax.dynamic_slice_in_dim(dv_acc, start, span, 0) + dv_win, start, 0)
        return ((dk_acc, dv_acc), dx_blk)
    (dk_acc, dv_acc), dx_rows = lax.scan(one_block, (zero_pad, zero_pad), jnp.arange(N_CTX, dtype=jnp.int32))
    grad_input = dx_rows.reshape(SEQ, D)
    grad_key = rms_back(k_float, key_gain, dk_acc[margin:]).astype(jnp.bfloat16).reshape(SEQ, KVH * HD)
    grad_value = dv_acc[margin:].astype(jnp.bfloat16).reshape(SEQ, KVH * HD)
    return (grad_input, grad_key, grad_value)
```

```python
import functools

import jax
import jax.numpy as jnp
from jax import lax
from jax.experimental import pallas as pl
from jax.experimental.pallas import tpu as pltpu
from jax.sharding import PartitionSpec as P

HD = 128
BLOCK = 128
HOPS = 10
NBUCKET = 16
PAIR = 2
BACK = HOPS // PAIR
NCH = BACK + 1
KEYS = PAIR * BLOCK
KVROWS = 2 * BLOCK + 16
EPS = 1e-06
MESH = pl.DeviceIdType.MESH
F32 = jnp.float32
BF16 = jnp.bfloat16
EXP2_SCALE = (HD**-0.5) * 1.4426950408889634


def dot(a, b):
    return jnp.dot(a, b, preferred_element_type=F32)


def dot_t(a, b):
    return lax.dot_general(a, b, (((0,), (0,)), ((), ())), preferred_element_type=F32)


def kernel(
    n_ctx,
    n_head,
    heads,
    bucket_ref,
    table_ref,
    doc_ref,
    qgain_ref,
    kgain_ref,
    q_hbm,
    k_hbm,
    v_hbm,
    g_hbm,
    w_hbm,
    gi_ref,
    gk_ref,
    gv_ref,
    q_ref,
    k_ref,
    v_ref,
    g_ref,
    w_ref,
    kvb,
    mask,
    qt,
    rq,
    qhat,
    qhat_t,
    g_t,
    gs,
    gs_t,
    delta,
    total,
    out_t,
    expo,
    ds,
    dq_t,
    dqr_t,
    part_tmp,
    part_own,
    part_out,
    part_in,
    comb,
    arrived,
    term_out,
    relay_in,
    term_in,
    in_sem,
    kv_send,
    kv_recv,
    fw_send,
    fw_recv,
    pt_send,
    pt_recv,
    cb_send,
    cb_recv,
    rs_send,
    rs_recv,
):
    me = lax.axis_index("ctx")
    hx = lax.axis_index("head")
    core = lax.rem(me, PAIR)
    sib = me + 1 - 2 * core
    other = 1 - core
    width = gi_ref.shape[1]
    half = width // 2
    pairs = heads // 2

    def ctx_at(step):
        return lax.rem(me + step * PAIR + n_ctx, n_ctx)

    def head_at(step):
        return lax.rem(hx + step + n_head, n_head)

    loads = [
        pltpu.make_async_copy(k_hbm, k_ref, in_sem.at[0]),
        pltpu.make_async_copy(v_hbm, v_ref, in_sem.at[1]),
        pltpu.make_async_copy(q_hbm, q_ref, in_sem.at[2]),
        pltpu.make_async_copy(g_hbm, g_ref, in_sem.at[3]),
        pltpu.make_async_copy(w_hbm, w_ref, in_sem.at[4]),
    ]
    for copy in loads:
        copy.start()

    barrier = pltpu.get_barrier_semaphore()
    peers = [(sib, hx), (me, head_at(1)), (me, head_at(-1))]
    for step in range(1, BACK + 1):
        peers += [(ctx_at(step), hx), (ctx_at(-step), hx)]
    for peer in peers:
        pl.semaphore_signal(barrier, inc=1, device_id=peer, device_id_type=MESH)

    own_doc = doc_ref[0].astype(F32)
    loads[0].wait()
    loads[1].wait()
    k_f = k_ref[...].astype(F32)
    k_r = lax.rsqrt(jnp.mean(k_f * k_f, axis=-1, keepdims=True) + EPS)
    kvb[0, core, 0:BLOCK, :] = (k_f * k_r * kgain_ref[...]).astype(BF16)
    kvb[0, core, BLOCK : 2 * BLOCK, :] = v_ref[...]
    kvb[0, core, 2 * BLOCK : KVROWS, :] = jnp.full((16, HD), own_doc, F32).astype(BF16)
    pl.semaphore_wait(barrier, len(peers))

    sends = []

    def send(src, dst, send_sem, recv_sem, target):
        copy = pltpu.make_async_remote_copy(
            src_ref=src,
            dst_ref=dst,
            send_sem=send_sem,
            recv_sem=recv_sem,
            device_id=target,
            device_id_type=MESH,
        )
        copy.start()
        sends.append(copy)
        return copy

    own_kv = kvb.at[0, core]
    fw = [send(own_kv, own_kv, fw_send.at[0], fw_recv.at[0], (sib, hx))]
    kv = [None]
    for j in range(1, NCH):
        kv.append(
            send(own_kv, kvb.at[j, core], kv_send.at[j], kv_recv.at[j], (ctx_at(j), hx))
        )

    weight = jnp.zeros((1, BLOCK), F32)
    for b in range(NBUCKET):
        weight = jnp.where(bucket_ref[...] == b, table_ref[b], weight)
    gain_t = jnp.broadcast_to(qgain_ref[...], (HD, HD)).T
    loads[2].wait()
    for h in range(heads):
        cols = pl.ds(h * HD, HD)
        x_t = q_ref[:, cols].T
        qt[cols, :] = x_t
        x = x_t.astype(F32)
        r = lax.rsqrt(jnp.mean(x * x, axis=0, keepdims=True) + EPS)
        rq[h : h + 1, :] = r
        hat = (x * r * gain_t).astype(BF16)
        qhat_t[:, cols] = hat
        qhat[cols, :] = hat.T
    loads[3].wait()
    for h in range(heads):
        cols = pl.ds(h * HD, HD)
        g_t[:, cols] = g_ref[:, cols].T

    key_pos = lax.broadcasted_iota(jnp.int32, (KEYS, BLOCK), 0)
    row_pos = lax.broadcasted_iota(jnp.int32, (KEYS, BLOCK), 1) + core * BLOCK
    causal = jnp.where(key_pos <= row_pos, 1.0, 0.0)

    for j in range(NCH):
        if j > 0:
            kv[j].wait_recv()
            slot = kvb.at[j, core]
            fw.append(send(slot, slot, fw_send.at[j], fw_recv.at[j], (sib, hx)))
        fw[j].wait_recv()
        for b in range(PAIR):
            docs = kvb[j, b, 2 * BLOCK : KVROWS, :].astype(F32)[0:1]
            same = jnp.where(docs == own_doc, 1.0, 0.0)
            rows = slice(b * BLOCK, (b + 1) * BLOCK)
            if j == 0:
                mask[rows, :] = causal[rows] * same
            else:
                mask[rows, :] = jnp.broadcast_to(same, (BLOCK, BLOCK))
        keys = jnp.concatenate([kvb[j, b, 0:BLOCK, :] for b in range(PAIR)], axis=0)
        vals = jnp.concatenate([kvb[j, b, BLOCK : 2 * BLOCK, :] for b in range(PAIR)], axis=0)
        for p in range(pairs):
            cols = pl.ds(p * KEYS, KEYS)
            s = dot(keys, qhat_t[:, cols])
            m = mask[...]
            e = jnp.exp2(s * EXP2_SCALE) * jnp.concatenate([m, m], axis=1)
            part = jnp.sum(e.reshape(KEYS // 8, 8, KEYS), axis=0)
            e_half = e.astype(BF16)
            expo[j, :, cols] = e_half
            weighted = dot_t(vals, e_half)
            if j == 0:
                total[:, cols] = part
                out_t[:, cols] = weighted
            else:
                total[:, cols] += part
                out_t[:, cols] += weighted

    for p in range(pairs):
        cols = pl.ds(p * KEYS, KEYS)
        inv = 1.0 / jnp.sum(total[:, cols], axis=0, keepdims=True)
        scaled = (g_t[:, cols].astype(F32) * (jnp.concatenate([weight, weight], axis=1) * inv)).astype(BF16)
        gs_t[:, cols] = scaled
        gs[cols, :] = scaled.T
        delta[:, cols] = jnp.broadcast_to(
            jnp.sum(scaled.astype(F32) * out_t[:, cols], axis=0, keepdims=True) * inv, (8, KEYS)
        )

    mine = pl.ds(pl.multiple_of(core * BLOCK, BLOCK), BLOCK)
    theirs = pl.ds(pl.multiple_of(other * BLOCK, BLOCK), BLOCK)
    pt = [None] * NCH
    cb = [None] * NCH

    def pass_on(j):
        pt[j].wait_recv()
        both = part_own[j] + part_in[j].astype(F32)
        if j > 0:
            comb[j] = both.astype(BF16)
            cb[j] = send(comb.at[j], arrived.at[j], cb_send.at[j], cb_recv.at[j], (ctx_at(-j), hx))
        else:
            part_own[0] = both

    order = list(range(NCH - 1, -1, -1))
    for n, j in enumerate(order):
        keys = jnp.concatenate([kvb[j, b, 0:BLOCK, :] for b in range(PAIR)], axis=0)
        vals = jnp.concatenate([kvb[j, b, BLOCK : 2 * BLOCK, :] for b in range(PAIR)], axis=0)
        for p in range(pairs):
            cols = pl.ds(p * KEYS, KEYS)
            gv = dot(vals, gs_t[:, cols])
            e = expo[j, :, cols].astype(F32)
            d = (e * (gv - delta[0:1, cols])).astype(BF16)
            ds[:, cols] = d
            dq = dot_t(keys, d)
            if n == 0:
                dq_t[:, cols] = dq
            else:
                dq_t[:, cols] += dq
        part_tmp[0] = dot(ds[...], qhat[...])
        part_tmp[1] = dot(expo[j], gs[...])
        for i in range(2):
            rows = slice(i * BLOCK, (i + 1) * BLOCK)
            part_own[j, rows, :] = part_tmp[i, mine, :]
            part_out[j, rows, :] = part_tmp[i, theirs, :].astype(BF16)
        pt[j] = send(part_out.at[j], part_in.at[j], pt_send.at[j], pt_recv.at[j], (sib, hx))
        if n > 0:
            pass_on(order[n - 1])

    for h in range(heads):
        cols = pl.ds(h * HD, HD)
        r = rq[h : h + 1, :]
        xn = qt[cols, :].astype(F32) * r
        gc = gain_t * (dq_t[:, cols] * (HD**-0.5))
        back = r * (gc - xn * jnp.mean(xn * gc, axis=0, keepdims=True))
        dqr_t[cols, :] = back.astype(BF16)

    loads[4].wait()

    def term(step, part):
        first = pl.multiple_of(head_at(step) * width + part * half, half)
        return dot(w_ref[pl.ds(first, half), :], dqr_t[...])

    def hand(slot, value, dst, recv, step):
        term_out[slot] = value.astype(BF16)
        return send(term_out.at[slot], dst, rs_send.at[slot], rs_recv.at[recv], (me, head_at(step)))

    up_relay = hand(0, term(2, 0), relay_in.at[0], 0, 1)
    down_relay = hand(1, term(2, 1), relay_in.at[1], 1, -1)
    direct_up = hand(2, term(1, 1), term_in.at[0, 1], 2, 1)
    direct_down = hand(3, term(-1, 0), term_in.at[1, 0], 3, -1)
    part = term(1, 0)
    up_relay.wait_recv()
    summed_up = hand(4, part + relay_in[0].astype(F32), term_in.at[0, 0], 4, 1)
    part = term(-1, 1)
    down_relay.wait_recv()
    summed_down = hand(5, part + relay_in[1].astype(F32), term_in.at[1, 1], 5, -1)
    own = [term(0, 0), term(0, 1)]

    pass_on(0)
    dkv = part_own[0]
    for j in range(NCH - 1, 0, -1):
        cb[j].wait_recv()
        dkv = dkv + arrived[j].astype(F32)
    gv_ref[...] = dkv[BLOCK:].astype(BF16)
    k_f = k_ref[...].astype(F32)
    k_r = lax.rsqrt(jnp.mean(k_f * k_f, axis=-1, keepdims=True) + EPS)
    xn = k_f * k_r
    gc = kgain_ref[...] * (dkv[:BLOCK] * (HD**-0.5))
    gk_ref[...] = (k_r * (gc - xn * jnp.mean(xn * gc, axis=-1, keepdims=True))).astype(BF16)

    for i, arrivals in enumerate(((summed_up, direct_down), (direct_up, summed_down))):
        for copy in arrivals:
            copy.wait_recv()
        sum_t = own[i] + term_in[0, i].astype(F32) + term_in[1, i].astype(F32)
        for b in range(half // BLOCK):
            first = i * half + b * BLOCK
            gi_ref[:, first : first + BLOCK] = sum_t[b * BLOCK : (b + 1) * BLOCK].T.astype(BF16)

    for copy in sends:
        copy.wait_send()


def local(mesh, *args):
    q, k, v, g, q_gain, k_gain, table, bucket, docs, w = args
    n_ctx, n_head = mesh.shape["ctx"], mesh.shape["head"]
    tokens, features = q.shape
    heads = features // HD
    cols = heads * BLOCK
    width = w.shape[0] // n_head
    half = width // 2
    vmem = pl.BlockSpec(memory_space=pltpu.VMEM)
    smem = pl.BlockSpec(memory_space=pltpu.SMEM)
    hbm = pl.BlockSpec(memory_space=pl.ANY)
    dma = pltpu.SemaphoreType.DMA
    return pl.pallas_call(
        functools.partial(kernel, n_ctx, n_head, heads),
        out_shape=(
            jax.ShapeDtypeStruct((tokens, width), BF16),
            jax.ShapeDtypeStruct(k.shape, BF16),
            jax.ShapeDtypeStruct(v.shape, BF16),
        ),
        in_specs=[vmem, smem, smem, vmem, vmem, hbm, hbm, hbm, hbm, hbm],
        out_specs=(vmem, vmem, vmem),
        scratch_shapes=[
            pltpu.VMEM(q.shape, BF16),
            pltpu.VMEM(k.shape, BF16),
            pltpu.VMEM(v.shape, BF16),
            pltpu.VMEM(g.shape, BF16),
            pltpu.VMEM(w.shape, BF16),
            pltpu.VMEM((NCH, PAIR, KVROWS, HD), BF16),
            pltpu.VMEM((KEYS, BLOCK), F32),
            pltpu.VMEM((cols, BLOCK), BF16),
            pltpu.VMEM((heads, BLOCK), F32),
            pltpu.VMEM((cols, HD), BF16),
            pltpu.VMEM((HD, cols), BF16),
            pltpu.VMEM((HD, cols), BF16),
            pltpu.VMEM((cols, HD), BF16),
            pltpu.VMEM((HD, cols), BF16),
            pltpu.VMEM((8, cols), F32),
            pltpu.VMEM((8, cols), F32),
            pltpu.VMEM((HD, cols), F32),
            pltpu.VMEM((NCH, KEYS, cols), BF16),
            pltpu.VMEM((KEYS, cols), BF16),
            pltpu.VMEM((HD, cols), F32),
            pltpu.VMEM((cols, BLOCK), BF16),
            pltpu.VMEM((2, KEYS, HD), F32),
            pltpu.VMEM((NCH, 2 * BLOCK, HD), F32),
            pltpu.VMEM((NCH, 2 * BLOCK, HD), BF16),
            pltpu.VMEM((NCH, 2 * BLOCK, HD), BF16),
            pltpu.VMEM((NCH, 2 * BLOCK, HD), BF16),
            pltpu.VMEM((NCH, 2 * BLOCK, HD), BF16),
            pltpu.VMEM((6, half, BLOCK), BF16),
            pltpu.VMEM((2, half, BLOCK), BF16),
            pltpu.VMEM((2, 2, half, BLOCK), BF16),
            dma((5,)),
            dma((NCH,)),
            dma((NCH,)),
            dma((NCH,)),
            dma((NCH,)),
            dma((NCH,)),
            dma((NCH,)),
            dma((NCH,)),
            dma((NCH,)),
            dma((6,)),
            dma((6,)),
        ],
        compiler_params=pltpu.CompilerParams(
            collective_id=0, has_side_effects=True, vmem_limit_bytes=56 * 1024 * 1024
        ),
    )(bucket.reshape(1, tokens), table, docs, q_gain.reshape(1, HD), k_gain.reshape(1, HD), q, k, v, g, w)


def solution(mesh):
    placed = (
        P("ctx", "head"),
        P("ctx", "head"),
        P("ctx", "head"),
        P("ctx", "head"),
        P(),
        P(),
        P(),
        P("ctx"),
        P("ctx"),
        P(None, "head"),
    )
    return jax.shard_map(
        functools.partial(local, mesh),
        mesh=mesh,
        in_specs=placed,
        out_specs=(P("ctx", "head"), P("ctx", "head"), P("ctx", "head")),
        check_vma=False,
    )
```

```python
import functools

import jax
import jax.numpy as jnp
from jax import lax
from jax.experimental import pallas as pl
from jax.experimental.pallas import tpu as pltpu
from jax.sharding import PartitionSpec as P

HD = 128
BLOCK = 128
HOPS = 10
NBUCKET = 16
PAIR = 2
BACK = HOPS // PAIR
NCH = BACK + 1
KEYS = PAIR * BLOCK
KVROWS = 2 * BLOCK + 16
EPS = 1e-06
MESH = pl.DeviceIdType.MESH
F32 = jnp.float32
BF16 = jnp.bfloat16
EXP2_SCALE = (HD**-0.5) * 1.4426950408889634


def dot(a, b):
    return jnp.dot(a, b, preferred_element_type=F32)


def dot_nt(a, b):
    return lax.dot_general(a, b, (((1,), (1,)), ((), ())), preferred_element_type=F32)


def dot_t(a, b):
    return lax.dot_general(a, b, (((0,), (0,)), ((), ())), preferred_element_type=F32)


def kernel(
    n_ctx,
    n_head,
    heads,
    bucket_ref,
    table_ref,
    doc_ref,
    qgain_ref,
    kgain_ref,
    q_hbm,
    k_hbm,
    v_hbm,
    g_hbm,
    w_hbm,
    gi_ref,
    gk_ref,
    gv_ref,
    doc_s,
    q_ref,
    k_ref,
    v_ref,
    g_ref,
    w_ref,
    kvb,
    mask,
    qt,
    rq,
    qhat_t,
    g_t,
    gs_t,
    rows_of,
    total,
    out_t,
    expo,
    prods,
    ds,
    dq_t,
    dqr_t,
    part_tmp,
    part_own,
    part_out,
    part_in,
    comb,
    arrived,
    term_out,
    relay_in,
    term_in,
    in_sem,
    kv_send,
    kv_recv,
    fw_send,
    fw_recv,
    pt_send,
    pt_recv,
    cb_send,
    cb_recv,
    rs_send,
    rs_recv,
):
    me = lax.axis_index("ctx")
    hx = lax.axis_index("head")
    core = lax.rem(me, PAIR)
    sib = me + 1 - 2 * core
    other = 1 - core
    width = gi_ref.shape[1]
    half = width // 2
    pairs = heads // 2

    chip = lax.div(me, PAIR)
    chips = n_ctx // PAIR

    def has_back(step):
        return chip >= step

    def has_next(step):
        return chip + step < chips

    def ctx_at(step):
        return me + step * PAIR

    def head_at(step):
        return lax.rem(hx + step + n_head, n_head)

    loads = [
        pltpu.make_async_copy(k_hbm, k_ref, in_sem.at[0]),
        pltpu.make_async_copy(v_hbm, v_ref, in_sem.at[1]),
        pltpu.make_async_copy(q_hbm, q_ref, in_sem.at[2]),
        pltpu.make_async_copy(g_hbm, g_ref, in_sem.at[3]),
        pltpu.make_async_copy(w_hbm, w_ref, in_sem.at[4]),
        pltpu.make_async_copy(doc_ref, doc_s, in_sem.at[5]),
    ]
    for i in (0, 1, 5, 2, 3, 4):
        loads[i].start()

    barrier = pltpu.get_barrier_semaphore()

    def greet(target):
        pl.semaphore_signal(barrier, inc=1, device_id=target, device_id_type=MESH)

    for peer in [(sib, hx), (me, head_at(1)), (me, head_at(-1))]:
        greet(peer)
    for step in range(1, BACK + 1):

        @pl.when(has_next(step))
        def _():
            greet((ctx_at(step), hx))

        @pl.when(has_back(step))
        def _():
            greet((ctx_at(-step), hx))

    loads[5].wait()
    own_doc = jnp.full((1, HD), doc_s[0], jnp.int32).astype(F32)
    loads[0].wait()
    loads[1].wait()
    k_f = k_ref[...].astype(F32)
    k_r = lax.rsqrt(jnp.mean(k_f * k_f, axis=-1, keepdims=True) + EPS)
    kvb[0, core, 0:BLOCK, :] = (k_f * k_r * kgain_ref[...]).astype(BF16)
    kvb[0, core, BLOCK : 2 * BLOCK, :] = v_ref[...]
    kvb[0, core, 2 * BLOCK : KVROWS, :] = jnp.broadcast_to(own_doc, (16, HD)).astype(BF16)
    pl.semaphore_wait(barrier, 3 + jnp.minimum(chip, BACK) + jnp.minimum(chips - 1 - chip, BACK))

    sends = []

    def remote(src, dst, send_sem, recv_sem, target):
        return pltpu.make_async_remote_copy(
            src_ref=src,
            dst_ref=dst,
            send_sem=send_sem,
            recv_sem=recv_sem,
            device_id=target,
            device_id_type=MESH,
        )

    def send(src, dst, send_sem, recv_sem, target):
        copy = remote(src, dst, send_sem, recv_sem, target)
        copy.start()
        sends.append((copy, None))
        return copy

    def send_if(cond, src, dst, send_sem, recv_sem, target):
        copy = remote(src, dst, send_sem, recv_sem, target)
        pl.when(cond)(copy.start)
        sends.append((copy, cond))
        return copy

    own_kv = kvb.at[0, core]
    fw = [send(own_kv, own_kv, fw_send.at[0], fw_recv.at[0], (sib, hx))]
    for j in range(1, NCH):
        slot = kvb.at[j, core]
        fw.append(remote(slot, slot, fw_send.at[j], fw_recv.at[j], (sib, hx)))
        sends.append((fw[j], has_back(j)))
    kv = [None]
    for j in range(1, NCH):
        kv.append(
            send_if(has_next(j), own_kv, kvb.at[j, core], kv_send.at[j], kv_recv.at[j], (ctx_at(j), hx))
        )

    weight = jnp.zeros((1, BLOCK), F32)
    for b in range(NBUCKET):
        weight = jnp.where(bucket_ref[...] == b, table_ref[b], weight)
    gain_t = jnp.broadcast_to(qgain_ref[...], (HD, HD)).T
    loads[2].wait()
    for h in range(heads):
        cols = pl.ds(h * HD, HD)
        x_t = q_ref[:, cols].T
        qt[cols, :] = x_t
        x = x_t.astype(F32)
        r = lax.rsqrt(jnp.mean(x * x, axis=0, keepdims=True) + EPS)
        rq[h : h + 1, :] = r
        qhat_t[:, cols] = (x * r * gain_t).astype(BF16)
    loads[3].wait()
    for h in range(heads):
        cols = pl.ds(h * HD, HD)
        g_t[:, cols] = g_ref[:, cols].T

    key_pos = lax.broadcasted_iota(jnp.int32, (KEYS, BLOCK), 0)
    row_pos = lax.broadcasted_iota(jnp.int32, (KEYS, BLOCK), 1) + core * BLOCK
    causal = jnp.where(key_pos <= row_pos, 1.0, 0.0)

    def both(j, first):
        return jnp.concatenate([kvb[j, b, first : first + BLOCK, :] for b in range(PAIR)], axis=0)

    def first_pass(j):
        if j > 0:
            kv[j].wait_recv()
            fw[j].start()
        fw[j].wait_recv()
        for b in range(PAIR):
            docs = kvb[j, b, 2 * BLOCK : KVROWS, :].astype(F32)[0:1]
            same = jnp.where(docs == own_doc, 1.0, 0.0)
            rows = slice(b * BLOCK, (b + 1) * BLOCK)
            if j == 0:
                mask[rows, :] = causal[rows] * same
            else:
                mask[rows, :] = jnp.broadcast_to(same, (BLOCK, BLOCK))
        keys, vals = both(j, 0), both(j, BLOCK)
        for p in range(pairs):
            cols = pl.ds(p * KEYS, KEYS)
            s = dot(keys, qhat_t[:, cols])
            m = mask[...]
            e = jnp.exp2(s * EXP2_SCALE) * jnp.concatenate([m, m], axis=1)
            part = jnp.sum(e.reshape(KEYS // 8, 8, KEYS), axis=0)
            e_half = e.astype(BF16)
            expo[j, :, cols] = e_half
            prods[j, :, cols] = dot(vals, g_t[:, cols])
            weighted = dot_t(vals, e_half)
            if j == 0:
                total[:, cols] = part
                out_t[:, cols] = weighted
            else:
                total[:, cols] += part
                out_t[:, cols] += weighted

    for j in range(NCH):
        if j == 0:
            first_pass(0)
        else:
            pl.when(has_back(j))(functools.partial(first_pass, j))

    for p in range(pairs):
        cols = pl.ds(p * KEYS, KEYS)
        inv = 1.0 / jnp.sum(total[:, cols], axis=0, keepdims=True)
        ratio = jnp.concatenate([weight, weight], axis=1) * inv
        g = g_t[:, cols].astype(F32)
        gs_t[:, cols] = (g * ratio).astype(BF16)
        rows_of[0:1, cols] = ratio
        rows_of[1:2, cols] = jnp.sum(g * out_t[:, cols], axis=0, keepdims=True) * (inv * ratio)

    def second_pass(j):
        keys = both(j, 0)
        for p in range(pairs):
            cols = pl.ds(p * KEYS, KEYS)
            e = expo[j, :, cols].astype(F32)
            d = (e * (prods[j, :, cols] * rows_of[0:1, cols] - rows_of[1:2, cols])).astype(BF16)
            ds[j, :, cols] = d
            dq = dot_t(keys, d)
            if j == 0:
                dq_t[:, cols] = dq
            else:
                dq_t[:, cols] += dq

    for j in range(NCH):
        if j == 0:
            second_pass(0)
        else:
            pl.when(has_back(j))(functools.partial(second_pass, j))

    for h in range(heads):
        cols = pl.ds(h * HD, HD)
        r = rq[h : h + 1, :]
        xn = qt[cols, :].astype(F32) * r
        gc = gain_t * (dq_t[:, cols] * (HD**-0.5))
        back = r * (gc - xn * jnp.mean(xn * gc, axis=0, keepdims=True))
        dqr_t[cols, :] = back.astype(BF16)

    loads[4].wait()

    def term(step, part):
        first = pl.multiple_of(head_at(step) * width + part * half, half)
        return dot(w_ref[pl.ds(first, half), :], dqr_t[...])

    def hand(slot, value, dst, recv, step):
        term_out[slot] = value.astype(BF16)
        return send(term_out.at[slot], dst, rs_send.at[slot], rs_recv.at[recv], (me, head_at(step)))

    mine = pl.ds(pl.multiple_of(core * BLOCK, BLOCK), BLOCK)
    theirs = pl.ds(pl.multiple_of(other * BLOCK, BLOCK), BLOCK)
    pt = [
        remote(part_out.at[j], part_in.at[j], pt_send.at[j], pt_recv.at[j], (sib, hx)) for j in range(NCH)
    ]
    cb = [None] + [
        remote(comb.at[j], arrived.at[j], cb_send.at[j], cb_recv.at[j], (ctx_at(-j), hx))
        for j in range(1, NCH)
    ]
    for j in range(NCH):
        always = None if j == 0 else has_back(j)
        sends.append((pt[j], always))
        if j > 0:
            sends.append((cb[j], always))

    def share(j):
        part_tmp[0] = dot_nt(qhat_t[...], ds[j])
        part_tmp[1] = dot_nt(gs_t[...], expo[j])
        for i in range(2):
            rows = slice(i * BLOCK, (i + 1) * BLOCK)
            part_own[j, rows, :] = part_tmp[i, :, mine]
            part_out[j, rows, :] = part_tmp[i, :, theirs].astype(BF16)
        pt[j].start()

    def pass_on(j):
        pt[j].wait_recv()
        summed = part_own[j] + part_in[j].astype(F32)
        if j > 0:
            comb[j] = summed.astype(BF16)
            cb[j].start()
        else:
            part_own[0] = summed

    def shares(chunks):
        for j in chunks:
            if j == 0:
                share(0)
            else:
                pl.when(has_back(j))(functools.partial(share, j))
            if j + 1 < NCH:
                pl.when(has_back(j + 1))(functools.partial(pass_on, j + 1))

    up_relay = hand(0, term(2, 0), relay_in.at[0], 0, 1)
    down_relay = hand(1, term(2, 1), relay_in.at[1], 1, -1)
    shares((5, 4, 3))
    direct_up = hand(2, term(1, 1), term_in.at[0, 1], 2, 1)
    direct_down = hand(3, term(-1, 0), term_in.at[1, 0], 3, -1)
    shares((2, 1, 0))
    part = term(1, 0)
    up_relay.wait_recv()
    summed_up = hand(4, part + relay_in[0].astype(F32), term_in.at[0, 0], 4, 1)
    part = term(-1, 1)
    down_relay.wait_recv()
    summed_down = hand(5, part + relay_in[1].astype(F32), term_in.at[1, 1], 5, -1)
    own = [term(0, 0), term(0, 1)]

    pass_on(0)
    for j in range(NCH - 1, 0, -1):

        @pl.when(has_next(j))
        def _():
            cb[j].wait_recv()
            part_own[0] += arrived[j].astype(F32)

    gv_ref[...] = part_own[0, BLOCK:, :].T.astype(BF16)
    k_f = k_ref[...].astype(F32)
    k_r = lax.rsqrt(jnp.mean(k_f * k_f, axis=-1, keepdims=True) + EPS)
    xn = k_f * k_r
    gc = kgain_ref[...] * (part_own[0, :BLOCK, :].T * (HD**-0.5))
    gk_ref[...] = (k_r * (gc - xn * jnp.mean(xn * gc, axis=-1, keepdims=True))).astype(BF16)

    for i, arrivals in enumerate(((summed_up, direct_down), (direct_up, summed_down))):
        for copy in arrivals:
            copy.wait_recv()
        sum_t = own[i] + term_in[0, i].astype(F32) + term_in[1, i].astype(F32)
        for b in range(half // BLOCK):
            first = i * half + b * BLOCK
            gi_ref[:, first : first + BLOCK] = sum_t[b * BLOCK : (b + 1) * BLOCK].T.astype(BF16)

    for copy, cond in sends:
        if cond is None:
            copy.wait_send()
        else:
            pl.when(cond)(copy.wait_send)


def hand_out(a, b, c, a_out, b_out, c_out, sem):
    copies = [
        pltpu.make_async_copy(src, dst, sem.at[i])
        for i, (src, dst) in enumerate(((a, a_out), (b, b_out), (c, c_out)))
    ]
    for copy in copies:
        copy.start()
    for copy in copies:
        copy.wait()


def local(mesh, *args):
    q, k, v, g, q_gain, k_gain, table, bucket, docs, w = args
    n_ctx, n_head = mesh.shape["ctx"], mesh.shape["head"]
    tokens, features = q.shape
    heads = features // HD
    cols = heads * BLOCK
    width = w.shape[0] // n_head
    half = width // 2
    vmem = pl.BlockSpec(memory_space=pltpu.VMEM)
    smem = pl.BlockSpec(memory_space=pltpu.SMEM)
    hbm = pl.BlockSpec(memory_space=pl.ANY)
    dma = pltpu.SemaphoreType.DMA
    results = pl.pallas_call(
        functools.partial(kernel, n_ctx, n_head, heads),
        out_shape=(
            pltpu.VMEM((tokens, width), BF16),
            pltpu.VMEM(k.shape, BF16),
            pltpu.VMEM(v.shape, BF16),
        ),
        in_specs=[vmem, smem, pl.BlockSpec(memory_space=pltpu.HBM), vmem, vmem, hbm, hbm, hbm, hbm, hbm],
        out_specs=(vmem, vmem, vmem),
        scratch_shapes=[
            pltpu.SMEM((1,), jnp.int32),
            pltpu.VMEM(q.shape, BF16),
            pltpu.VMEM(k.shape, BF16),
            pltpu.VMEM(v.shape, BF16),
            pltpu.VMEM(g.shape, BF16),
            pltpu.VMEM(w.shape, BF16),
            pltpu.VMEM((NCH, PAIR, KVROWS, HD), BF16),
            pltpu.VMEM((KEYS, BLOCK), F32),
            pltpu.VMEM((cols, BLOCK), BF16),
            pltpu.VMEM((heads, BLOCK), F32),
            pltpu.VMEM((HD, cols), BF16),
            pltpu.VMEM((HD, cols), BF16),
            pltpu.VMEM((HD, cols), BF16),
            pltpu.VMEM((8, cols), F32),
            pltpu.VMEM((8, cols), F32),
            pltpu.VMEM((HD, cols), F32),
            pltpu.VMEM((NCH, KEYS, cols), BF16),
            pltpu.VMEM((NCH, KEYS, cols), F32),
            pltpu.VMEM((NCH, KEYS, cols), BF16),
            pltpu.VMEM((HD, cols), F32),
            pltpu.VMEM((cols, BLOCK), BF16),
            pltpu.VMEM((2, HD, KEYS), F32),
            pltpu.VMEM((NCH, 2 * BLOCK, HD), F32),
            pltpu.VMEM((NCH, 2 * BLOCK, HD), BF16),
            pltpu.VMEM((NCH, 2 * BLOCK, HD), BF16),
            pltpu.VMEM((NCH, 2 * BLOCK, HD), BF16),
            pltpu.VMEM((NCH, 2 * BLOCK, HD), BF16),
            pltpu.VMEM((6, half, BLOCK), BF16),
            pltpu.VMEM((2, half, BLOCK), BF16),
            pltpu.VMEM((2, 2, half, BLOCK), BF16),
            dma((6,)),
            dma((NCH,)),
            dma((NCH,)),
            dma((NCH,)),
            dma((NCH,)),
            dma((NCH,)),
            dma((NCH,)),
            dma((NCH,)),
            dma((NCH,)),
            dma((6,)),
            dma((6,)),
        ],
        compiler_params=pltpu.CompilerParams(
            collective_id=0, has_side_effects=True, vmem_limit_bytes=56 * 1024 * 1024
        ),
    )(bucket.reshape(1, tokens), table, docs, q_gain.reshape(1, HD), k_gain.reshape(1, HD), q, k, v, g, w)
    return pl.pallas_call(
        hand_out,
        out_shape=tuple(jax.ShapeDtypeStruct(r.shape, r.dtype) for r in results),
        in_specs=[vmem] * 3,
        out_specs=(hbm,) * 3,
        scratch_shapes=[dma((3,))],
    )(*(pltpu.with_memory_space_constraint(r, pltpu.VMEM) for r in results))


def solution(mesh):
    placed = (
        P("ctx", "head"),
        P("ctx", "head"),
        P("ctx", "head"),
        P("ctx", "head"),
        P(),
        P(),
        P(),
        P("ctx"),
        P("ctx"),
        P(None, "head"),
    )
    return jax.shard_map(
        functools.partial(local, mesh),
        mesh=mesh,
        in_specs=placed,
        out_specs=(P("ctx", "head"), P("ctx", "head"), P("ctx", "head")),
        check_vma=False,
    )
```

```python
import functools

import jax
import jax.numpy as jnp
from jax import lax
from jax.experimental import pallas as pl
from jax.experimental.pallas import tpu as pltpu
from jax.sharding import PartitionSpec as P

HD = 128
BLOCK = 128
HOPS = 10
NBUCKET = 16
PAIR = 2
BACK = HOPS // PAIR
NCH = BACK + 1
KEYS = PAIR * BLOCK
KVROWS = 2 * BLOCK + 16
EPS = 1e-06
MESH = pl.DeviceIdType.MESH
F32 = jnp.float32
BF16 = jnp.bfloat16
EXP2_SCALE = (HD**-0.5) * 1.4426950408889634


def dot(a, b):
    return jnp.dot(a, b, preferred_element_type=F32)


def dot_nt(a, b):
    return lax.dot_general(a, b, (((1,), (1,)), ((), ())), preferred_element_type=F32)


def dot_t(a, b):
    return lax.dot_general(a, b, (((0,), (0,)), ((), ())), preferred_element_type=F32)


def kernel(
    n_ctx,
    n_head,
    heads,
    bucket_hbm,
    table_hbm,
    doc_hbm,
    qgain_hbm,
    kgain_hbm,
    q_hbm,
    k_hbm,
    v_hbm,
    g_hbm,
    w_hbm,
    gi_ref,
    gk_ref,
    gv_ref,
    bucket_ref,
    table_ref,
    doc_ref,
    qgain_ref,
    kgain_ref,
    q_ref,
    k_ref,
    v_ref,
    g_ref,
    w_ref,
    kvb,
    mask,
    qt,
    rq,
    qhat_t,
    g_t,
    gs_t,
    rows_of,
    total,
    out_t,
    expo,
    prods,
    ds,
    dq_t,
    dqr_t,
    part_tmp,
    part_own,
    part_out,
    part_in,
    comb,
    arrived,
    term_out,
    relay_in,
    term_in,
    own,
    in_sem,
    kv_send,
    kv_recv,
    fw_send,
    fw_recv,
    pt_send,
    pt_recv,
    cb_send,
    cb_recv,
    rs_send,
    rs_recv,
):
    me = lax.axis_index("ctx")
    hx = lax.axis_index("head")
    core = lax.rem(me, PAIR)
    sib = me + 1 - 2 * core
    other = 1 - core
    width = gi_ref.shape[1]
    quarter = width // 4
    pairs = heads // 2

    chip = lax.div(me, PAIR)
    chips = n_ctx // PAIR

    def has_back(step):
        return chip >= step

    def has_next(step):
        return chip + step < chips

    def ctx_at(step):
        return me + step * PAIR

    def head_at(step):
        return lax.rem(hx + step + n_head, n_head)

    barrier = pltpu.get_barrier_semaphore()

    def greet(target):
        pl.semaphore_signal(barrier, inc=1, device_id=target, device_id_type=MESH)

    for peer in [(sib, hx), (me, head_at(1)), (me, head_at(-1))]:
        greet(peer)
    for step in range(1, BACK + 1):

        @pl.when(has_back(step))
        def _():
            greet((ctx_at(-step), hx))

    loads = [
        pltpu.make_async_copy(src, dst, in_sem.at[i])
        for i, (src, dst) in enumerate(
            (
                (k_hbm, k_ref),
                (v_hbm, v_ref),
                (kgain_hbm, kgain_ref),
                (doc_hbm, doc_ref),
                (q_hbm, q_ref),
                (qgain_hbm, qgain_ref),
                (table_hbm, table_ref),
                (bucket_hbm, bucket_ref),
                (g_hbm, g_ref),
                (w_hbm, w_ref),
            )
        )
    ]
    for copy in loads:
        copy.start()

    for copy in loads[:4]:
        copy.wait()
    own_doc = jnp.full((1, HD), doc_ref[0], jnp.int32).astype(F32)
    k_f = k_ref[...].astype(F32)
    k_r = lax.rsqrt(jnp.mean(k_f * k_f, axis=-1, keepdims=True) + EPS)
    kvb[0, core, 0:BLOCK, :] = (k_f * k_r * kgain_ref[...]).astype(BF16)
    kvb[0, core, BLOCK : 2 * BLOCK, :] = v_ref[...]
    kvb[0, core, 2 * BLOCK : KVROWS, :] = jnp.broadcast_to(own_doc, (16, HD)).astype(BF16)
    pl.semaphore_wait(barrier, 3 + jnp.minimum(chips - 1 - chip, BACK))

    sends = []

    def remote(src, dst, send_sem, recv_sem, target):
        return pltpu.make_async_remote_copy(
            src_ref=src,
            dst_ref=dst,
            send_sem=send_sem,
            recv_sem=recv_sem,
            device_id=target,
            device_id_type=MESH,
        )

    def send(src, dst, send_sem, recv_sem, target):
        copy = remote(src, dst, send_sem, recv_sem, target)
        copy.start()
        sends.append((copy, None))
        return copy

    def send_if(cond, src, dst, send_sem, recv_sem, target):
        copy = remote(src, dst, send_sem, recv_sem, target)
        pl.when(cond)(copy.start)
        sends.append((copy, cond))
        return copy

    own_kv = kvb.at[0, core]
    fw = [send(own_kv, own_kv, fw_send.at[0], fw_recv.at[0], (sib, hx))]
    for j in range(1, NCH):
        slot = kvb.at[j, core]
        fw.append(remote(slot, slot, fw_send.at[j], fw_recv.at[j], (sib, hx)))
        sends.append((fw[j], has_back(j)))
    kv = [None]
    for j in range(1, NCH):
        kv.append(
            send_if(has_next(j), own_kv, kvb.at[j, core], kv_send.at[j], kv_recv.at[j], (ctx_at(j), hx))
        )

    for copy in loads[4:8]:
        copy.wait()
    weight = jnp.zeros((1, BLOCK), F32)
    for b in range(NBUCKET):
        weight = jnp.where(bucket_ref[...] == b, table_ref[b], weight)
    gain_t = jnp.broadcast_to(qgain_ref[...], (HD, HD)).T
    for h in range(heads):
        cols = pl.ds(h * HD, HD)
        x_t = q_ref[:, cols].T
        qt[cols, :] = x_t
        x = x_t.astype(F32)
        r = lax.rsqrt(jnp.mean(x * x, axis=0, keepdims=True) + EPS)
        rq[h : h + 1, :] = r
        qhat_t[:, cols] = (x * r * gain_t).astype(BF16)
    loads[8].wait()
    for h in range(heads):
        cols = pl.ds(h * HD, HD)
        g_t[:, cols] = g_ref[:, cols].T

    key_pos = lax.broadcasted_iota(jnp.int32, (KEYS, BLOCK), 0)
    row_pos = lax.broadcasted_iota(jnp.int32, (KEYS, BLOCK), 1) + core * BLOCK
    causal = jnp.where(key_pos <= row_pos, 1.0, 0.0)

    def both(j, first):
        return jnp.concatenate([kvb[j, b, first : first + BLOCK, :] for b in range(PAIR)], axis=0)

    def first_pass(j):
        if j > 0:
            kv[j].wait_recv()
            fw[j].start()
        fw[j].wait_recv()
        for b in range(PAIR):
            docs = kvb[j, b, 2 * BLOCK : KVROWS, :].astype(F32)[0:1]
            same = jnp.where(docs == own_doc, 1.0, 0.0)
            rows = slice(b * BLOCK, (b + 1) * BLOCK)
            if j == 0:
                mask[rows, :] = causal[rows] * same
            else:
                mask[rows, :] = jnp.broadcast_to(same, (BLOCK, BLOCK))
        keys, vals = both(j, 0), both(j, BLOCK)
        for p in range(pairs):
            cols = pl.ds(p * KEYS, KEYS)
            s = dot(keys, qhat_t[:, cols])
            m = mask[...]
            e = jnp.exp2(s * EXP2_SCALE) * jnp.concatenate([m, m], axis=1)
            part = jnp.sum(e.reshape(KEYS // 8, 8, KEYS), axis=0)
            e_half = e.astype(BF16)
            expo[j, :, cols] = e_half
            prods[j, :, cols] = dot(vals, g_t[:, cols])
            weighted = dot_t(vals, e_half)
            if j == 0:
                total[:, cols] = part
                out_t[:, cols] = weighted
            else:
                total[:, cols] += part
                out_t[:, cols] += weighted

    for j in range(NCH):
        if j == 0:
            first_pass(0)
        else:
            pl.when(has_back(j))(functools.partial(first_pass, j))

    for p in range(pairs):
        cols = pl.ds(p * KEYS, KEYS)
        inv = 1.0 / jnp.sum(total[:, cols], axis=0, keepdims=True)
        ratio = jnp.concatenate([weight, weight], axis=1) * inv
        g = g_t[:, cols].astype(F32)
        gs_t[:, cols] = (g * ratio).astype(BF16)
        rows_of[0:1, cols] = ratio
        rows_of[1:2, cols] = jnp.sum(g * out_t[:, cols], axis=0, keepdims=True) * (inv * ratio)

    def second_pass(j):
        keys = both(j, 0)
        for p in range(pairs):
            cols = pl.ds(p * KEYS, KEYS)
            e = expo[j, :, cols].astype(F32)
            d = (e * (prods[j, :, cols] * rows_of[0:1, cols] - rows_of[1:2, cols])).astype(BF16)
            ds[j, :, cols] = d
            dq = dot_t(keys, d)
            if j == 0:
                dq_t[:, cols] = dq
            else:
                dq_t[:, cols] += dq

    for j in range(NCH):
        if j == 0:
            second_pass(0)
        else:
            pl.when(has_back(j))(functools.partial(second_pass, j))

    for h in range(heads):
        cols = pl.ds(h * HD, HD)
        r = rq[h : h + 1, :]
        xn = qt[cols, :].astype(F32) * r
        gc = gain_t * (dq_t[:, cols] * (HD**-0.5))
        back = r * (gc - xn * jnp.mean(xn * gc, axis=0, keepdims=True))
        dqr_t[cols, :] = back.astype(BF16)

    loads[9].wait()

    def term(step, part):
        first = pl.multiple_of(head_at(step) * width + part * quarter, quarter)
        return dot(w_ref[pl.ds(first, quarter), :], dqr_t[...])

    def hand(slot, value, dst, step):
        term_out[slot] = value.astype(BF16)
        return send(term_out.at[slot], dst, rs_send.at[slot], rs_recv.at[slot], (me, head_at(step)))

    def relay(side, q):
        part = term(2, q + 2 * side)
        return hand(side * 6 + q, part, relay_in.at[side, q], 1 - 2 * side)

    def direct(side, q):
        at = q + 2 - 2 * side
        part = term(1 - 2 * side, at)
        return hand(side * 6 + 2 + q, part, term_in.at[side, at], 1 - 2 * side)

    def summed(side, q, arriving):
        at = q + 2 * side
        part = term(1 - 2 * side, at)
        arriving.wait_recv()
        part = part + relay_in[side, q].astype(F32)
        return hand(side * 6 + 4 + q, part, term_in.at[side, at], 1 - 2 * side)

    mine = pl.ds(pl.multiple_of(core * BLOCK, BLOCK), BLOCK)
    theirs = pl.ds(pl.multiple_of(other * BLOCK, BLOCK), BLOCK)
    pt = [
        remote(part_out.at[j], part_in.at[j], pt_send.at[j], pt_recv.at[j], (sib, hx)) for j in range(NCH)
    ]
    cb = [None] + [
        remote(comb.at[j], arrived.at[j], cb_send.at[j], cb_recv.at[j], (ctx_at(-j), hx))
        for j in range(1, NCH)
    ]
    for j in range(NCH):
        always = None if j == 0 else has_back(j)
        sends.append((pt[j], always))
        if j > 0:
            sends.append((cb[j], always))

    def share(j):
        part_tmp[0] = dot_nt(qhat_t[...], ds[j])
        part_tmp[1] = dot_nt(gs_t[...], expo[j])
        for i in range(2):
            rows = slice(i * BLOCK, (i + 1) * BLOCK)
            part_own[j, rows, :] = part_tmp[i, :, mine]
            part_out[j, rows, :] = part_tmp[i, :, theirs].astype(BF16)
        pt[j].start()

    def pass_on(j):
        pt[j].wait_recv()
        summed = part_own[j] + part_in[j].astype(F32)
        if j > 0:
            comb[j] = summed.astype(BF16)
            cb[j].start()
        else:
            part_own[0] = summed

    def shares(chunks):
        for j in chunks:
            if j == 0:
                share(0)
            else:
                pl.when(has_back(j))(functools.partial(share, j))
            if j + 1 < NCH:
                pl.when(has_back(j + 1))(functools.partial(pass_on, j + 1))

    relayed = {(side, q): relay(side, q) for q in range(2) for side in range(2)}
    shares((5, 4))
    straight = {(side, q): direct(side, q) for q in range(2) for side in range(2)}
    shares((3, 2))
    added = {(side, q): summed(side, q, relayed[side, q]) for q in range(2) for side in range(2)}
    shares((1, 0))
    for q in range(4):
        own[q] = term(0, q)

    pass_on(0)
    for j in range(NCH - 1, 0, -1):

        @pl.when(has_next(j))
        def _():
            cb[j].wait_recv()
            part_own[0] += arrived[j].astype(F32)

    gv_ref[...] = part_own[0, BLOCK:, :].T.astype(BF16)
    k_f = k_ref[...].astype(F32)
    k_r = lax.rsqrt(jnp.mean(k_f * k_f, axis=-1, keepdims=True) + EPS)
    xn = k_f * k_r
    gc = kgain_ref[...] * (part_own[0, :BLOCK, :].T * (HD**-0.5))
    gk_ref[...] = (k_r * (gc - xn * jnp.mean(xn * gc, axis=-1, keepdims=True))).astype(BF16)

    for q, arrivals in (
        (0, (added[0, 0], straight[1, 0])),
        (2, (straight[0, 0], added[1, 0])),
        (1, (added[0, 1], straight[1, 1])),
        (3, (straight[0, 1], added[1, 1])),
    ):
        for copy in arrivals:
            copy.wait_recv()
        sum_t = (own[q] + term_in[0, q].astype(F32) + term_in[1, q].astype(F32)).astype(BF16)
        for b in range(quarter // BLOCK):
            first = q * quarter + b * BLOCK
            gi_ref[:, first : first + BLOCK] = sum_t[b * BLOCK : (b + 1) * BLOCK].T

    for copy, cond in sends:
        if cond is None:
            copy.wait_send()
        else:
            pl.when(cond)(copy.wait_send)


def hand_out(a, b, c, a_out, b_out, c_out, sem):
    copies = [
        pltpu.make_async_copy(src, dst, sem.at[i])
        for i, (src, dst) in enumerate(((a, a_out), (b, b_out), (c, c_out)))
    ]
    for copy in copies:
        copy.start()
    for copy in copies:
        copy.wait()


def local(mesh, *args):
    q, k, v, g, q_gain, k_gain, table, bucket, docs, w = args
    n_ctx, n_head = mesh.shape["ctx"], mesh.shape["head"]
    tokens, features = q.shape
    heads = features // HD
    cols = heads * BLOCK
    width = w.shape[0] // n_head
    quarter = width // 4
    vmem = pl.BlockSpec(memory_space=pltpu.VMEM)
    smem = pl.BlockSpec(memory_space=pltpu.SMEM)
    hbm = pl.BlockSpec(memory_space=pl.ANY)
    dma = pltpu.SemaphoreType.DMA
    results = pl.pallas_call(
        functools.partial(kernel, n_ctx, n_head, heads),
        out_shape=(
            pltpu.VMEM((tokens, width), BF16),
            pltpu.VMEM(k.shape, BF16),
            pltpu.VMEM(v.shape, BF16),
        ),
        in_specs=[hbm, pl.BlockSpec(memory_space=pltpu.HBM), pl.BlockSpec(memory_space=pltpu.HBM)] + [hbm] * 7,
        out_specs=(vmem, vmem, vmem),
        scratch_shapes=[
            pltpu.VMEM((1, tokens), jnp.int32),
            pltpu.SMEM((NBUCKET,), F32),
            pltpu.SMEM((1,), jnp.int32),
            pltpu.VMEM((1, HD), F32),
            pltpu.VMEM((1, HD), F32),
            pltpu.VMEM(q.shape, BF16),
            pltpu.VMEM(k.shape, BF16),
            pltpu.VMEM(v.shape, BF16),
            pltpu.VMEM(g.shape, BF16),
            pltpu.VMEM(w.shape, BF16),
            pltpu.VMEM((NCH, PAIR, KVROWS, HD), BF16),
            pltpu.VMEM((KEYS, BLOCK), F32),
            pltpu.VMEM((cols, BLOCK), BF16),
            pltpu.VMEM((heads, BLOCK), F32),
            pltpu.VMEM((HD, cols), BF16),
            pltpu.VMEM((HD, cols), BF16),
            pltpu.VMEM((HD, cols), BF16),
            pltpu.VMEM((8, cols), F32),
            pltpu.VMEM((8, cols), F32),
            pltpu.VMEM((HD, cols), F32),
            pltpu.VMEM((NCH, KEYS, cols), BF16),
            pltpu.VMEM((NCH, KEYS, cols), F32),
            pltpu.VMEM((NCH, KEYS, cols), BF16),
            pltpu.VMEM((HD, cols), F32),
            pltpu.VMEM((cols, BLOCK), BF16),
            pltpu.VMEM((2, HD, KEYS), F32),
            pltpu.VMEM((NCH, 2 * BLOCK, HD), F32),
            pltpu.VMEM((NCH, 2 * BLOCK, HD), BF16),
            pltpu.VMEM((NCH, 2 * BLOCK, HD), BF16),
            pltpu.VMEM((NCH, 2 * BLOCK, HD), BF16),
            pltpu.VMEM((NCH, 2 * BLOCK, HD), BF16),
            pltpu.VMEM((12, quarter, BLOCK), BF16),
            pltpu.VMEM((2, 2, quarter, BLOCK), BF16),
            pltpu.VMEM((2, 4, quarter, BLOCK), BF16),
            pltpu.VMEM((4, quarter, BLOCK), F32),
            dma((10,)),
            dma((NCH,)),
            dma((NCH,)),
            dma((NCH,)),
            dma((NCH,)),
            dma((NCH,)),
            dma((NCH,)),
            dma((NCH,)),
            dma((NCH,)),
            dma((12,)),
            dma((12,)),
        ],
        compiler_params=pltpu.CompilerParams(
            collective_id=0, has_side_effects=True, vmem_limit_bytes=56 * 1024 * 1024
        ),
    )(bucket.reshape(1, tokens), table, docs, q_gain.reshape(1, HD), k_gain.reshape(1, HD), q, k, v, g, w)
    return pl.pallas_call(
        hand_out,
        out_shape=tuple(jax.ShapeDtypeStruct(r.shape, r.dtype) for r in results),
        in_specs=[vmem] * 3,
        out_specs=(hbm,) * 3,
        scratch_shapes=[dma((3,))],
    )(*(pltpu.with_memory_space_constraint(r, pltpu.VMEM) for r in results))


def solution(mesh):
    placed = (
        P("ctx", "head"),
        P("ctx", "head"),
        P("ctx", "head"),
        P("ctx", "head"),
        P(),
        P(),
        P(),
        P("ctx"),
        P("ctx"),
        P(None, "head"),
    )
    return jax.shard_map(
        functools.partial(local, mesh),
        mesh=mesh,
        in_specs=placed,
        out_specs=(P("ctx", "head"), P("ctx", "head"), P("ctx", "head")),
        check_vma=False,
    )
```

```python
import functools

import jax
import jax.numpy as jnp
from jax import lax
from jax.experimental import pallas as pl
from jax.experimental.pallas import tpu as pltpu
from jax.sharding import PartitionSpec as P

HD = 128
BLOCK = 128
HOPS = 10
NBUCKET = 16
PAIR = 2
BACK = HOPS // PAIR
NCH = BACK + 1
ROW = 4
ORDER = (0, 4, 1, 2, 3, 5)
KEYS = PAIR * BLOCK
KVROWS = 2 * BLOCK + 16
EPS = 1e-06
MESH = pl.DeviceIdType.MESH
F32 = jnp.float32
BF16 = jnp.bfloat16
EXP2_SCALE = (HD**-0.5) * 1.4426950408889634


def dot(a, b):
    return jnp.dot(a, b, preferred_element_type=F32)


def dot_nt(a, b):
    return lax.dot_general(a, b, (((1,), (1,)), ((), ())), preferred_element_type=F32)


def dot_t(a, b):
    return lax.dot_general(a, b, (((0,), (0,)), ((), ())), preferred_element_type=F32)


def kernel(
    n_ctx,
    n_head,
    heads,
    bucket_hbm,
    table_hbm,
    doc_hbm,
    qgain_hbm,
    kgain_hbm,
    q_hbm,
    k_hbm,
    v_hbm,
    g_hbm,
    w_hbm,
    gi_ref,
    gk_ref,
    gv_ref,
    bucket_ref,
    table_ref,
    doc_ref,
    qgain_ref,
    kgain_ref,
    q_ref,
    k_ref,
    v_ref,
    g_ref,
    w_ref,
    kvb,
    mask,
    qt,
    rq,
    qhat_t,
    g_t,
    gs_t,
    rows_of,
    total,
    out_t,
    expo,
    prods,
    ds,
    dq_t,
    dqr_t,
    part_tmp,
    part_own,
    part_out,
    part_in,
    comb,
    arrived,
    term_out,
    relay_in,
    term_in,
    own,
    in_sem,
    kv_send,
    kv_recv,
    rl_send,
    fw_send,
    fw_recv,
    pt_send,
    pt_recv,
    cb_send,
    cb_recv,
    rs_send,
    rs_recv,
):
    me = lax.axis_index("ctx")
    hx = lax.axis_index("head")
    core = lax.rem(me, PAIR)
    sib = me + 1 - 2 * core
    other = 1 - core
    width = gi_ref.shape[1]
    quarter = width // 4
    pairs = heads // 2

    chip = lax.div(me, PAIR)
    chips = n_ctx // PAIR
    place = lax.rem(chip, ROW)

    def has_back(step):
        return chip >= step

    def has_next(step):
        return chip + step < chips

    def ctx_at(step):
        return me + step * PAIR

    def head_at(step):
        return lax.rem(hx + step + n_head, n_head)

    barrier = pltpu.get_barrier_semaphore()

    def greet(target):
        pl.semaphore_signal(barrier, inc=1, device_id=target, device_id_type=MESH)

    for peer in [(sib, hx), (me, head_at(1)), (me, head_at(-1))]:
        greet(peer)
    for step in range(1, ROW):
        greet((ctx_at(lax.rem(place + step, ROW) - place), hx))

    @pl.when(has_back(ROW))
    def _():
        greet((ctx_at(-ROW), hx))

    starts_row = place == 0
    ends_row = place == ROW - 1

    @pl.when(jnp.logical_and(starts_row, has_back(1)))
    def _():
        greet((ctx_at(-1), hx))

    loads = [
        pltpu.make_async_copy(src, dst, in_sem.at[i])
        for i, (src, dst) in enumerate(
            (
                (k_hbm, k_ref),
                (v_hbm, v_ref),
                (kgain_hbm, kgain_ref),
                (doc_hbm, doc_ref),
                (q_hbm, q_ref),
                (qgain_hbm, qgain_ref),
                (table_hbm, table_ref),
                (bucket_hbm, bucket_ref),
                (g_hbm, g_ref),
                (w_hbm, w_ref),
            )
        )
    ]
    for copy in loads:
        copy.start()

    for copy in loads[:4]:
        copy.wait()
    own_doc = jnp.full((1, HD), doc_ref[0], jnp.int32).astype(F32)
    k_f = k_ref[...].astype(F32)
    k_r = lax.rsqrt(jnp.mean(k_f * k_f, axis=-1, keepdims=True) + EPS)
    kvb[0, core, 0:BLOCK, :] = (k_f * k_r * kgain_ref[...]).astype(BF16)
    kvb[0, core, BLOCK : 2 * BLOCK, :] = v_ref[...]
    kvb[0, core, 2 * BLOCK : KVROWS, :] = jnp.broadcast_to(own_doc, (16, HD)).astype(BF16)
    awaited = 3 + ROW - 1 + jnp.where(has_next(ROW), 1, 0) + jnp.where(jnp.logical_and(ends_row, has_next(1)), 1, 0)
    pl.semaphore_wait(barrier, awaited)

    sends = []

    def remote(src, dst, send_sem, recv_sem, target):
        return pltpu.make_async_remote_copy(
            src_ref=src,
            dst_ref=dst,
            send_sem=send_sem,
            recv_sem=recv_sem,
            device_id=target,
            device_id_type=MESH,
        )

    def send(src, dst, send_sem, recv_sem, target):
        copy = remote(src, dst, send_sem, recv_sem, target)
        copy.start()
        sends.append((copy, None))
        return copy

    def send_if(cond, src, dst, send_sem, recv_sem, target):
        copy = remote(src, dst, send_sem, recv_sem, target)
        pl.when(cond)(copy.start)
        sends.append((copy, cond))
        return copy

    own_kv = kvb.at[0, core]
    fw = [send(own_kv, own_kv, fw_send.at[0], fw_recv.at[0], (sib, hx))]
    for j in range(1, NCH):
        slot = kvb.at[j, core]
        fw.append(remote(slot, slot, fw_send.at[j], fw_recv.at[j], (sib, hx)))
        sends.append((fw[j], has_back(j)))
    for step in range(1, ROW):
        send_if(
            place + step < ROW, own_kv, kvb.at[step, core], kv_send.at[step], kv_recv.at[step], (ctx_at(step), hx)
        )
    send_if(
        has_next(ROW), own_kv, kvb.at[ROW, core], kv_send.at[ROW], kv_recv.at[ROW], (ctx_at(ROW), hx)
    )
    kv = [None]
    for j in range(1, NCH):
        slot = kvb.at[j, core]
        kv.append(remote(slot, slot, kv_send.at[j], kv_recv.at[j], (sib, hx)))
    relays = []
    for i, (step, cond) in enumerate(
        ((1, has_next(1)), (-1, place >= 1), (-2, place >= 2), (-3, place >= 3))
    ):
        far = ROW + step
        relays.append(
            (
                cond,
                remote(
                    kvb.at[ROW, core], kvb.at[far, core], rl_send.at[i], kv_recv.at[far], (ctx_at(step), hx)
                ),
            )
        )
        sends.append((relays[i][1], jnp.logical_and(cond, has_back(ROW))))

    for copy in loads[4:8]:
        copy.wait()
    weight = jnp.zeros((1, BLOCK), F32)
    for b in range(NBUCKET):
        weight = jnp.where(bucket_ref[...] == b, table_ref[b], weight)
    gain_t = jnp.broadcast_to(qgain_ref[...], (HD, HD)).T
    for h in range(heads):
        cols = pl.ds(h * HD, HD)
        x_t = q_ref[:, cols].T
        qt[cols, :] = x_t
        x = x_t.astype(F32)
        r = lax.rsqrt(jnp.mean(x * x, axis=0, keepdims=True) + EPS)
        rq[h : h + 1, :] = r
        qhat_t[:, cols] = (x * r * gain_t).astype(BF16)
    loads[8].wait()
    for h in range(heads):
        cols = pl.ds(h * HD, HD)
        g_t[:, cols] = g_ref[:, cols].T

    key_pos = lax.broadcasted_iota(jnp.int32, (KEYS, BLOCK), 0)
    row_pos = lax.broadcasted_iota(jnp.int32, (KEYS, BLOCK), 1) + core * BLOCK
    causal = jnp.where(key_pos <= row_pos, 1.0, 0.0)

    def both(j, first):
        return jnp.concatenate([kvb[j, b, first : first + BLOCK, :] for b in range(PAIR)], axis=0)

    def fetch(j):
        @pl.when(has_back(j))
        def _():
            kv[j].wait_recv()
            if j == ROW:
                for cond, copy in relays:
                    pl.when(cond)(copy.start)
            fw[j].start()

    def first_pass(j, following):
        fw[j].wait_recv()
        for b in range(PAIR):
            docs = kvb[j, b, 2 * BLOCK : KVROWS, :].astype(F32)[0:1]
            same = jnp.where(docs == own_doc, 1.0, 0.0)
            rows = slice(b * BLOCK, (b + 1) * BLOCK)
            if j == 0:
                mask[rows, :] = causal[rows] * same
            else:
                mask[rows, :] = jnp.broadcast_to(same, (BLOCK, BLOCK))
        keys, vals = both(j, 0), both(j, BLOCK)
        for p in range(pairs):
            cols = pl.ds(p * KEYS, KEYS)
            s = dot(keys, qhat_t[:, cols])
            m = mask[...]
            e = jnp.exp2(s * EXP2_SCALE) * jnp.concatenate([m, m], axis=1)
            part = jnp.sum(e.reshape(KEYS // 8, 8, KEYS), axis=0)
            e_half = e.astype(BF16)
            expo[j, :, cols] = e_half
            prods[j, :, cols] = dot(vals, g_t[:, cols])
            weighted = dot_t(vals, e_half)
            if j == 0:
                total[:, cols] = part
                out_t[:, cols] = weighted
            else:
                total[:, cols] += part
                out_t[:, cols] += weighted
            if p == 0 and following is not None:
                fetch(following)

    for j, following in zip(ORDER, ORDER[1:] + (None,)):
        if j == 0:
            first_pass(0, following)
        else:
            pl.when(has_back(j))(functools.partial(first_pass, j, following))
            if following is not None:
                pl.when(jnp.logical_not(has_back(j)))(functools.partial(fetch, following))

    for p in range(pairs):
        cols = pl.ds(p * KEYS, KEYS)
        inv = 1.0 / jnp.sum(total[:, cols], axis=0, keepdims=True)
        ratio = jnp.concatenate([weight, weight], axis=1) * inv
        g = g_t[:, cols].astype(F32)
        gs_t[:, cols] = (g * ratio).astype(BF16)
        rows_of[0:1, cols] = ratio
        rows_of[1:2, cols] = jnp.sum(g * out_t[:, cols], axis=0, keepdims=True) * (inv * ratio)

    def second_pass(j):
        keys = both(j, 0)
        for p in range(pairs):
            cols = pl.ds(p * KEYS, KEYS)
            e = expo[j, :, cols].astype(F32)
            d = (e * (prods[j, :, cols] * rows_of[0:1, cols] - rows_of[1:2, cols])).astype(BF16)
            ds[j, :, cols] = d
            dq = dot_t(keys, d)
            if j == 0:
                dq_t[:, cols] = dq
            else:
                dq_t[:, cols] += dq

    for j in range(NCH):
        if j == 0:
            second_pass(0)
        else:
            pl.when(has_back(j))(functools.partial(second_pass, j))

    for h in range(heads):
        cols = pl.ds(h * HD, HD)
        r = rq[h : h + 1, :]
        xn = qt[cols, :].astype(F32) * r
        gc = gain_t * (dq_t[:, cols] * (HD**-0.5))
        back = r * (gc - xn * jnp.mean(xn * gc, axis=0, keepdims=True))
        dqr_t[cols, :] = back.astype(BF16)

    loads[9].wait()

    def term(step, part):
        first = pl.multiple_of(head_at(step) * width + part * quarter, quarter)
        return dot(w_ref[pl.ds(first, quarter), :], dqr_t[...])

    def hand(slot, value, dst, step):
        term_out[slot] = value.astype(BF16)
        return send(term_out.at[slot], dst, rs_send.at[slot], rs_recv.at[slot], (me, head_at(step)))

    def relay(side, q):
        part = term(2, q + 2 * side)
        return hand(side * 6 + q, part, relay_in.at[side, q], 1 - 2 * side)

    def direct(side, q):
        at = q + 2 - 2 * side
        part = term(1 - 2 * side, at)
        return hand(side * 6 + 2 + q, part, term_in.at[side, at], 1 - 2 * side)

    def summed(side, q, arriving):
        at = q + 2 * side
        part = term(1 - 2 * side, at)
        arriving.wait_recv()
        part = part + relay_in[side, q].astype(F32)
        return hand(side * 6 + 4 + q, part, term_in.at[side, at], 1 - 2 * side)

    mine = pl.ds(pl.multiple_of(core * BLOCK, BLOCK), BLOCK)
    theirs = pl.ds(pl.multiple_of(other * BLOCK, BLOCK), BLOCK)
    pt = [
        remote(part_out.at[j], part_in.at[j], pt_send.at[j], pt_recv.at[j], (sib, hx)) for j in range(NCH)
    ]
    cb = [None] + [
        remote(comb.at[j], arrived.at[j], cb_send.at[j], cb_recv.at[j], (ctx_at(-j), hx))
        for j in range(1, NCH)
    ]
    for j in range(NCH):
        always = None if j == 0 else has_back(j)
        sends.append((pt[j], always))
        if j > 0:
            sends.append((cb[j], always))

    def share(j):
        part_tmp[0] = dot_nt(qhat_t[...], ds[j])
        part_tmp[1] = dot_nt(gs_t[...], expo[j])
        for i in range(2):
            rows = slice(i * BLOCK, (i + 1) * BLOCK)
            part_own[j, rows, :] = part_tmp[i, :, mine]
            part_out[j, rows, :] = part_tmp[i, :, theirs].astype(BF16)
        pt[j].start()

    def pass_on(j):
        pt[j].wait_recv()
        summed = part_own[j] + part_in[j].astype(F32)
        if j > 0:
            comb[j] = summed.astype(BF16)
            cb[j].start()
        else:
            part_own[0] = summed

    def shares(chunks):
        for j in chunks:
            if j == 0:
                share(0)
            else:
                pl.when(has_back(j))(functools.partial(share, j))
            if j + 1 < NCH:
                pl.when(has_back(j + 1))(functools.partial(pass_on, j + 1))

    relayed = {(side, q): relay(side, q) for q in range(2) for side in range(2)}
    shares((5, 4))
    straight = {(side, q): direct(side, q) for q in range(2) for side in range(2)}
    shares((3, 2))
    added = {(side, q): summed(side, q, relayed[side, q]) for q in range(2) for side in range(2)}
    shares((1, 0))
    for q in range(4):
        own[q] = term(0, q)

    pass_on(0)
    for j in range(NCH - 1, 0, -1):

        @pl.when(has_next(j))
        def _():
            cb[j].wait_recv()
            part_own[0] += arrived[j].astype(F32)

    gv_ref[...] = part_own[0, BLOCK:, :].T.astype(BF16)
    k_f = k_ref[...].astype(F32)
    k_r = lax.rsqrt(jnp.mean(k_f * k_f, axis=-1, keepdims=True) + EPS)
    xn = k_f * k_r
    gc = kgain_ref[...] * (part_own[0, :BLOCK, :].T * (HD**-0.5))
    gk_ref[...] = (k_r * (gc - xn * jnp.mean(xn * gc, axis=-1, keepdims=True))).astype(BF16)

    for q, arrivals in (
        (0, (added[0, 0], straight[1, 0])),
        (2, (straight[0, 0], added[1, 0])),
        (1, (added[0, 1], straight[1, 1])),
        (3, (straight[0, 1], added[1, 1])),
    ):
        for copy in arrivals:
            copy.wait_recv()
        sum_t = (own[q] + term_in[0, q].astype(F32) + term_in[1, q].astype(F32)).astype(BF16)
        for b in range(quarter // BLOCK):
            first = q * quarter + b * BLOCK
            gi_ref[:, first : first + BLOCK] = sum_t[b * BLOCK : (b + 1) * BLOCK].T

    for copy, cond in sends:
        if cond is None:
            copy.wait_send()
        else:
            pl.when(cond)(copy.wait_send)


def hand_out(a, b, c, a_out, b_out, c_out, sem):
    copies = [
        pltpu.make_async_copy(src, dst, sem.at[i])
        for i, (src, dst) in enumerate(((a, a_out), (b, b_out), (c, c_out)))
    ]
    for copy in copies:
        copy.start()
    for copy in copies:
        copy.wait()


def local(mesh, *args):
    q, k, v, g, q_gain, k_gain, table, bucket, docs, w = args
    n_ctx, n_head = mesh.shape["ctx"], mesh.shape["head"]
    tokens, features = q.shape
    heads = features // HD
    cols = heads * BLOCK
    width = w.shape[0] // n_head
    quarter = width // 4
    vmem = pl.BlockSpec(memory_space=pltpu.VMEM)
    smem = pl.BlockSpec(memory_space=pltpu.SMEM)
    hbm = pl.BlockSpec(memory_space=pl.ANY)
    dma = pltpu.SemaphoreType.DMA
    results = pl.pallas_call(
        functools.partial(kernel, n_ctx, n_head, heads),
        out_shape=(
            pltpu.VMEM((tokens, width), BF16),
            pltpu.VMEM(k.shape, BF16),
            pltpu.VMEM(v.shape, BF16),
        ),
        in_specs=[hbm, pl.BlockSpec(memory_space=pltpu.HBM), pl.BlockSpec(memory_space=pltpu.HBM)] + [hbm] * 7,
        out_specs=(vmem, vmem, vmem),
        scratch_shapes=[
            pltpu.VMEM((1, tokens), jnp.int32),
            pltpu.SMEM((NBUCKET,), F32),
            pltpu.SMEM((1,), jnp.int32),
            pltpu.VMEM((1, HD), F32),
            pltpu.VMEM((1, HD), F32),
            pltpu.VMEM(q.shape, BF16),
            pltpu.VMEM(k.shape, BF16),
            pltpu.VMEM(v.shape, BF16),
            pltpu.VMEM(g.shape, BF16),
            pltpu.VMEM(w.shape, BF16),
            pltpu.VMEM((NCH, PAIR, KVROWS, HD), BF16),
            pltpu.VMEM((KEYS, BLOCK), F32),
            pltpu.VMEM((cols, BLOCK), BF16),
            pltpu.VMEM((heads, BLOCK), F32),
            pltpu.VMEM((HD, cols), BF16),
            pltpu.VMEM((HD, cols), BF16),
            pltpu.VMEM((HD, cols), BF16),
            pltpu.VMEM((8, cols), F32),
            pltpu.VMEM((8, cols), F32),
            pltpu.VMEM((HD, cols), F32),
            pltpu.VMEM((NCH, KEYS, cols), BF16),
            pltpu.VMEM((NCH, KEYS, cols), F32),
            pltpu.VMEM((NCH, KEYS, cols), BF16),
            pltpu.VMEM((HD, cols), F32),
            pltpu.VMEM((cols, BLOCK), BF16),
            pltpu.VMEM((2, HD, KEYS), F32),
            pltpu.VMEM((NCH, 2 * BLOCK, HD), F32),
            pltpu.VMEM((NCH, 2 * BLOCK, HD), BF16),
            pltpu.VMEM((NCH, 2 * BLOCK, HD), BF16),
            pltpu.VMEM((NCH, 2 * BLOCK, HD), BF16),
            pltpu.VMEM((NCH, 2 * BLOCK, HD), BF16),
            pltpu.VMEM((12, quarter, BLOCK), BF16),
            pltpu.VMEM((2, 2, quarter, BLOCK), BF16),
            pltpu.VMEM((2, 4, quarter, BLOCK), BF16),
            pltpu.VMEM((4, quarter, BLOCK), F32),
            dma((10,)),
            dma((NCH,)),
            dma((NCH,)),
            dma((4,)),
            dma((NCH,)),
            dma((NCH,)),
            dma((NCH,)),
            dma((NCH,)),
            dma((NCH,)),
            dma((NCH,)),
            dma((12,)),
            dma((12,)),
        ],
        compiler_params=pltpu.CompilerParams(
            collective_id=0, has_side_effects=True, vmem_limit_bytes=56 * 1024 * 1024
        ),
    )(bucket.reshape(1, tokens), table, docs, q_gain.reshape(1, HD), k_gain.reshape(1, HD), q, k, v, g, w)
    return pl.pallas_call(
        hand_out,
        out_shape=tuple(jax.ShapeDtypeStruct(r.shape, r.dtype) for r in results),
        in_specs=[vmem] * 3,
        out_specs=(hbm,) * 3,
        scratch_shapes=[dma((3,))],
    )(*(pltpu.with_memory_space_constraint(r, pltpu.VMEM) for r in results))


def solution(mesh):
    placed = (
        P("ctx", "head"),
        P("ctx", "head"),
        P("ctx", "head"),
        P("ctx", "head"),
        P(),
        P(),
        P(),
        P("ctx"),
        P("ctx"),
        P(None, "head"),
    )
    return jax.shard_map(
        functools.partial(local, mesh),
        mesh=mesh,
        in_specs=placed,
        out_specs=(P("ctx", "head"), P("ctx", "head"), P("ctx", "head")),
        check_vma=False,
    )
```

```python
import functools

import jax
import jax.numpy as jnp
from jax import lax
from jax.experimental import pallas as pl
from jax.experimental.pallas import tpu as pltpu
from jax.sharding import PartitionSpec as P

HD = 128
BLOCK = 128
HOPS = 10
NBUCKET = 16
PAIR = 2
BACK = HOPS // PAIR
NCH = BACK + 1
KEYS = PAIR * BLOCK
KVROWS = 2 * BLOCK + 16
EPS = 1e-06
MESH = pl.DeviceIdType.MESH
F32 = jnp.float32
BF16 = jnp.bfloat16
EXP2_SCALE = (HD**-0.5) * 1.4426950408889634


def dot(a, b):
    return jnp.dot(a, b, preferred_element_type=F32)


def dot_nt(a, b):
    return lax.dot_general(a, b, (((1,), (1,)), ((), ())), preferred_element_type=F32)


def dot_t(a, b):
    return lax.dot_general(a, b, (((0,), (0,)), ((), ())), preferred_element_type=F32)


def kernel(
    n_ctx,
    n_head,
    heads,
    bucket_hbm,
    table_hbm,
    doc_hbm,
    qgain_hbm,
    kgain_hbm,
    q_hbm,
    k_hbm,
    v_hbm,
    g_hbm,
    w_hbm,
    gi_ref,
    gk_ref,
    gv_ref,
    bucket_ref,
    table_ref,
    doc_ref,
    qgain_ref,
    kgain_ref,
    q_ref,
    k_ref,
    v_ref,
    g_ref,
    w_ref,
    kvb,
    mask,
    qt,
    rq,
    qhat_t,
    g_t,
    gs_t,
    rows_of,
    total,
    out_t,
    expo,
    prods,
    ds,
    dq_t,
    dqr_t,
    part_tmp,
    part_own,
    part_out,
    part_in,
    comb,
    arrived,
    term_out,
    relay_in,
    term_in,
    own,
    in_sem,
    kv_send,
    kv_recv,
    fw_send,
    fw_recv,
    pt_send,
    pt_recv,
    cb_send,
    cb_recv,
    rs_send,
    rs_recv,
):
    me = lax.axis_index("ctx")
    hx = lax.axis_index("head")
    core = lax.rem(me, PAIR)
    sib = me + 1 - 2 * core
    other = 1 - core
    width = gi_ref.shape[1]
    quarter = width // 4
    pairs = heads // 2

    chip = lax.div(me, PAIR)
    chips = n_ctx // PAIR

    def has_back(step):
        return chip >= step

    def has_next(step):
        return chip + step < chips

    def ctx_at(step):
        return me + step * PAIR

    def head_at(step):
        return lax.rem(hx + step + n_head, n_head)

    barrier = pltpu.get_barrier_semaphore()

    def greet(target):
        pl.semaphore_signal(barrier, inc=1, device_id=target, device_id_type=MESH)

    for peer in [(sib, hx), (me, head_at(1)), (me, head_at(-1))]:
        greet(peer)
    for step in range(1, BACK + 1):

        @pl.when(has_back(step))
        def _():
            greet((ctx_at(-step), hx))

    loads = [
        pltpu.make_async_copy(src, dst, in_sem.at[i])
        for i, (src, dst) in enumerate(
            (
                (k_hbm, k_ref),
                (v_hbm, v_ref),
                (kgain_hbm, kgain_ref),
                (doc_hbm, doc_ref),
                (q_hbm, q_ref),
                (qgain_hbm, qgain_ref),
                (table_hbm, table_ref),
                (bucket_hbm, bucket_ref),
                (g_hbm, g_ref),
                (w_hbm, w_ref),
            )
        )
    ]
    for copy in loads:
        copy.start()

    for copy in loads[:4]:
        copy.wait()
    own_doc = jnp.full((1, HD), doc_ref[0], jnp.int32).astype(F32)
    k_f = k_ref[...].astype(F32)
    k_r = lax.rsqrt(jnp.mean(k_f * k_f, axis=-1, keepdims=True) + EPS)
    kvb[0, core, 0:BLOCK, :] = (k_f * k_r * kgain_ref[...]).astype(BF16)
    kvb[0, core, BLOCK : 2 * BLOCK, :] = v_ref[...]
    kvb[0, core, 2 * BLOCK : KVROWS, :] = jnp.broadcast_to(own_doc, (16, HD)).astype(BF16)
    pl.semaphore_wait(barrier, 3 + jnp.minimum(chips - 1 - chip, BACK))

    sends = []

    def remote(src, dst, send_sem, recv_sem, target):
        return pltpu.make_async_remote_copy(
            src_ref=src,
            dst_ref=dst,
            send_sem=send_sem,
            recv_sem=recv_sem,
            device_id=target,
            device_id_type=MESH,
        )

    def send(src, dst, send_sem, recv_sem, target):
        copy = remote(src, dst, send_sem, recv_sem, target)
        copy.start()
        sends.append((copy, None))
        return copy

    def send_if(cond, src, dst, send_sem, recv_sem, target):
        copy = remote(src, dst, send_sem, recv_sem, target)
        pl.when(cond)(copy.start)
        sends.append((copy, cond))
        return copy

    own_kv = kvb.at[0, core]
    fw = [send(own_kv, own_kv, fw_send.at[0], fw_recv.at[0], (sib, hx))]
    for j in range(1, NCH):
        slot = kvb.at[j, core]
        fw.append(remote(slot, slot, fw_send.at[j], fw_recv.at[j], (sib, hx)))
        sends.append((fw[j], has_back(j)))
    kv = [None]
    for j in range(1, NCH):
        kv.append(
            send_if(has_next(j), own_kv, kvb.at[j, core], kv_send.at[j], kv_recv.at[j], (ctx_at(j), hx))
        )

    for copy in loads[4:8]:
        copy.wait()
    weight = jnp.zeros((1, BLOCK), F32)
    for b in range(NBUCKET):
        weight = jnp.where(bucket_ref[...] == b, table_ref[b], weight)
    gain_t = jnp.broadcast_to(qgain_ref[...], (HD, HD)).T
    for h in range(heads):
        cols = pl.ds(h * HD, HD)
        x_t = q_ref[:, cols].T
        qt[cols, :] = x_t
        x = x_t.astype(F32)
        r = lax.rsqrt(jnp.mean(x * x, axis=0, keepdims=True) + EPS)
        rq[h : h + 1, :] = r
        qhat_t[:, cols] = (x * r * gain_t).astype(BF16)
    loads[8].wait()
    for h in range(heads):
        cols = pl.ds(h * HD, HD)
        g_t[:, cols] = g_ref[:, cols].T

    key_pos = lax.broadcasted_iota(jnp.int32, (KEYS, BLOCK), 0)
    row_pos = lax.broadcasted_iota(jnp.int32, (KEYS, BLOCK), 1) + core * BLOCK
    causal = jnp.where(key_pos <= row_pos, 1.0, 0.0)

    def both(j, first):
        return jnp.concatenate([kvb[j, b, first : first + BLOCK, :] for b in range(PAIR)], axis=0)

    def fetch(j):
        @pl.when(has_back(j))
        def _():
            kv[j].wait_recv()
            fw[j].start()

    def first_pass(j):
        fw[j].wait_recv()
        for b in range(PAIR):
            docs = kvb[j, b, 2 * BLOCK : KVROWS, :].astype(F32)[0:1]
            same = jnp.where(docs == own_doc, 1.0, 0.0)
            rows = slice(b * BLOCK, (b + 1) * BLOCK)
            if j == 0:
                mask[rows, :] = causal[rows] * same
            else:
                mask[rows, :] = jnp.broadcast_to(same, (BLOCK, BLOCK))
        keys, vals = both(j, 0), both(j, BLOCK)
        for p in range(pairs):
            cols = pl.ds(p * KEYS, KEYS)
            s = dot(keys, qhat_t[:, cols])
            m = mask[...]
            e = jnp.exp2(s * EXP2_SCALE) * jnp.concatenate([m, m], axis=1)
            part = jnp.sum(e.reshape(KEYS // 8, 8, KEYS), axis=0)
            e_half = e.astype(BF16)
            expo[j, :, cols] = e_half
            prods[j, :, cols] = dot(vals, g_t[:, cols])
            weighted = dot_t(vals, e_half)
            if j == 0:
                total[:, cols] = part
                out_t[:, cols] = weighted
            else:
                total[:, cols] += part
                out_t[:, cols] += weighted
            if p == pairs - 2 and j + 1 < NCH:
                fetch(j + 1)

    for j in range(NCH):
        if j == 0:
            first_pass(0)
        else:
            pl.when(has_back(j))(functools.partial(first_pass, j))

    for p in range(pairs):
        cols = pl.ds(p * KEYS, KEYS)
        inv = 1.0 / jnp.sum(total[:, cols], axis=0, keepdims=True)
        ratio = jnp.concatenate([weight, weight], axis=1) * inv
        g = g_t[:, cols].astype(F32)
        gs_t[:, cols] = (g * ratio).astype(BF16)
        rows_of[0:1, cols] = ratio
        rows_of[1:2, cols] = jnp.sum(g * out_t[:, cols], axis=0, keepdims=True) * (inv * ratio)

    def second_pass(j):
        keys = both(j, 0)
        for p in range(pairs):
            cols = pl.ds(p * KEYS, KEYS)
            e = expo[j, :, cols].astype(F32)
            d = (e * (prods[j, :, cols] * rows_of[0:1, cols] - rows_of[1:2, cols])).astype(BF16)
            ds[j, :, cols] = d
            dq = dot_t(keys, d)
            if j == 0:
                dq_t[:, cols] = dq
            else:
                dq_t[:, cols] += dq

    for j in range(NCH):
        if j == 0:
            second_pass(0)
        else:
            pl.when(has_back(j))(functools.partial(second_pass, j))

    for h in range(heads):
        cols = pl.ds(h * HD, HD)
        r = rq[h : h + 1, :]
        xn = qt[cols, :].astype(F32) * r
        gc = gain_t * (dq_t[:, cols] * (HD**-0.5))
        back = r * (gc - xn * jnp.mean(xn * gc, axis=0, keepdims=True))
        dqr_t[cols, :] = back.astype(BF16)

    loads[9].wait()

    def term(step, part):
        first = pl.multiple_of(head_at(step) * width + part * quarter, quarter)
        return dot(w_ref[pl.ds(first, quarter), :], dqr_t[...])

    def hand(slot, value, dst, step):
        term_out[slot] = value.astype(BF16)
        return send(term_out.at[slot], dst, rs_send.at[slot], rs_recv.at[slot], (me, head_at(step)))

    def relay(side, q):
        part = term(2, q + 2 * side)
        return hand(side * 6 + q, part, relay_in.at[side, q], 1 - 2 * side)

    def direct(side, q):
        at = q + 2 - 2 * side
        part = term(1 - 2 * side, at)
        return hand(side * 6 + 2 + q, part, term_in.at[side, at], 1 - 2 * side)

    def summed(side, q, arriving):
        at = q + 2 * side
        part = term(1 - 2 * side, at)
        arriving.wait_recv()
        part = part + relay_in[side, q].astype(F32)
        return hand(side * 6 + 4 + q, part, term_in.at[side, at], 1 - 2 * side)

    mine = pl.ds(pl.multiple_of(core * BLOCK, BLOCK), BLOCK)
    theirs = pl.ds(pl.multiple_of(other * BLOCK, BLOCK), BLOCK)
    pt = [
        remote(part_out.at[j], part_in.at[j], pt_send.at[j], pt_recv.at[j], (sib, hx)) for j in range(NCH)
    ]
    cb = [None] + [
        remote(comb.at[j], arrived.at[j], cb_send.at[j], cb_recv.at[j], (ctx_at(-j), hx))
        for j in range(1, NCH)
    ]
    for j in range(NCH):
        always = None if j == 0 else has_back(j)
        sends.append((pt[j], always))
        if j > 0:
            sends.append((cb[j], always))

    def share(j):
        part_tmp[0] = dot_nt(qhat_t[...], ds[j])
        part_tmp[1] = dot_nt(gs_t[...], expo[j])
        for i in range(2):
            rows = slice(i * BLOCK, (i + 1) * BLOCK)
            part_own[j, rows, :] = part_tmp[i, :, mine]
            part_out[j, rows, :] = part_tmp[i, :, theirs].astype(BF16)
        pt[j].start()

    def pass_on(j):
        pt[j].wait_recv()
        summed = part_own[j] + part_in[j].astype(F32)
        if j > 0:
            comb[j] = summed.astype(BF16)
            cb[j].start()
        else:
            part_own[0] = summed

    def shares(chunks):
        for j in chunks:
            pl.when(has_back(j))(functools.partial(share, j))
            if j + 1 < NCH:
                pl.when(has_back(j + 1))(functools.partial(pass_on, j + 1))

    relayed = {(side, q): relay(side, q) for q in range(2) for side in range(2)}
    shares((5, 4))
    straight = {(side, q): direct(side, q) for q in range(2) for side in range(2)}
    shares((3, 2, 1))
    added = {(side, 0): summed(side, 0, relayed[side, 0]) for side in range(2)}
    pl.when(has_back(1))(functools.partial(pass_on, 1))
    added |= {(side, 1): summed(side, 1, relayed[side, 1]) for side in range(2)}
    share(0)
    for q in range(4):
        own[q] = term(0, q)

    pass_on(0)
    for j in range(NCH - 1, 0, -1):

        @pl.when(has_next(j))
        def _():
            cb[j].wait_recv()
            part_own[0] += arrived[j].astype(F32)

    gv_ref[...] = part_own[0, BLOCK:, :].T.astype(BF16)
    k_f = k_ref[...].astype(F32)
    k_r = lax.rsqrt(jnp.mean(k_f * k_f, axis=-1, keepdims=True) + EPS)
    xn = k_f * k_r
    gc = kgain_ref[...] * (part_own[0, :BLOCK, :].T * (HD**-0.5))
    gk_ref[...] = (k_r * (gc - xn * jnp.mean(xn * gc, axis=-1, keepdims=True))).astype(BF16)

    for q, arrivals in (
        (0, (added[0, 0], straight[1, 0])),
        (2, (straight[0, 0], added[1, 0])),
        (1, (added[0, 1], straight[1, 1])),
        (3, (straight[0, 1], added[1, 1])),
    ):
        for copy in arrivals:
            copy.wait_recv()
        sum_t = (own[q] + term_in[0, q].astype(F32) + term_in[1, q].astype(F32)).astype(BF16)
        for b in range(quarter // BLOCK):
            first = q * quarter + b * BLOCK
            gi_ref[:, first : first + BLOCK] = sum_t[b * BLOCK : (b + 1) * BLOCK].T

    for copy, cond in sends:
        if cond is None:
            copy.wait_send()
        else:
            pl.when(cond)(copy.wait_send)


def hand_out(a, b, c, a_out, b_out, c_out, sem):
    copies = [
        pltpu.make_async_copy(src, dst, sem.at[i])
        for i, (src, dst) in enumerate(((a, a_out), (b, b_out), (c, c_out)))
    ]
    for copy in copies:
        copy.start()
    for copy in copies:
        copy.wait()


def local(mesh, *args):
    q, k, v, g, q_gain, k_gain, table, bucket, docs, w = args
    n_ctx, n_head = mesh.shape["ctx"], mesh.shape["head"]
    tokens, features = q.shape
    heads = features // HD
    cols = heads * BLOCK
    width = w.shape[0] // n_head
    quarter = width // 4
    vmem = pl.BlockSpec(memory_space=pltpu.VMEM)
    smem = pl.BlockSpec(memory_space=pltpu.SMEM)
    hbm = pl.BlockSpec(memory_space=pl.ANY)
    dma = pltpu.SemaphoreType.DMA
    results = pl.pallas_call(
        functools.partial(kernel, n_ctx, n_head, heads),
        out_shape=(
            pltpu.VMEM((tokens, width), BF16),
            pltpu.VMEM(k.shape, BF16),
            pltpu.VMEM(v.shape, BF16),
        ),
        in_specs=[hbm, pl.BlockSpec(memory_space=pltpu.HBM), pl.BlockSpec(memory_space=pltpu.HBM)] + [hbm] * 7,
        out_specs=(vmem, vmem, vmem),
        scratch_shapes=[
            pltpu.VMEM((1, tokens), jnp.int32),
            pltpu.SMEM((NBUCKET,), F32),
            pltpu.SMEM((1,), jnp.int32),
            pltpu.VMEM((1, HD), F32),
            pltpu.VMEM((1, HD), F32),
            pltpu.VMEM(q.shape, BF16),
            pltpu.VMEM(k.shape, BF16),
            pltpu.VMEM(v.shape, BF16),
            pltpu.VMEM(g.shape, BF16),
            pltpu.VMEM(w.shape, BF16),
            pltpu.VMEM((NCH, PAIR, KVROWS, HD), BF16),
            pltpu.VMEM((KEYS, BLOCK), F32),
            pltpu.VMEM((cols, BLOCK), BF16),
            pltpu.VMEM((heads, BLOCK), F32),
            pltpu.VMEM((HD, cols), BF16),
            pltpu.VMEM((HD, cols), BF16),
            pltpu.VMEM((HD, cols), BF16),
            pltpu.VMEM((8, cols), F32),
            pltpu.VMEM((8, cols), F32),
            pltpu.VMEM((HD, cols), F32),
            pltpu.VMEM((NCH, KEYS, cols), BF16),
            pltpu.VMEM((NCH, KEYS, cols), F32),
            pltpu.VMEM((NCH, KEYS, cols), BF16),
            pltpu.VMEM((HD, cols), F32),
            pltpu.VMEM((cols, BLOCK), BF16),
            pltpu.VMEM((2, HD, KEYS), F32),
            pltpu.VMEM((NCH, 2 * BLOCK, HD), F32),
            pltpu.VMEM((NCH, 2 * BLOCK, HD), BF16),
            pltpu.VMEM((NCH, 2 * BLOCK, HD), BF16),
            pltpu.VMEM((NCH, 2 * BLOCK, HD), BF16),
            pltpu.VMEM((NCH, 2 * BLOCK, HD), BF16),
            pltpu.VMEM((12, quarter, BLOCK), BF16),
            pltpu.VMEM((2, 2, quarter, BLOCK), BF16),
            pltpu.VMEM((2, 4, quarter, BLOCK), BF16),
            pltpu.VMEM((4, quarter, BLOCK), F32),
            dma((10,)),
            dma((NCH,)),
            dma((NCH,)),
            dma((NCH,)),
            dma((NCH,)),
            dma((NCH,)),
            dma((NCH,)),
            dma((NCH,)),
            dma((NCH,)),
            dma((12,)),
            dma((12,)),
        ],
        compiler_params=pltpu.CompilerParams(
            collective_id=0, has_side_effects=True, vmem_limit_bytes=56 * 1024 * 1024
        ),
    )(bucket.reshape(1, tokens), table, docs, q_gain.reshape(1, HD), k_gain.reshape(1, HD), q, k, v, g, w)
    return pl.pallas_call(
        hand_out,
        out_shape=tuple(jax.ShapeDtypeStruct(r.shape, r.dtype) for r in results),
        in_specs=[vmem] * 3,
        out_specs=(hbm,) * 3,
        scratch_shapes=[dma((3,))],
    )(*(pltpu.with_memory_space_constraint(r, pltpu.VMEM) for r in results))


def solution(mesh):
    placed = (
        P("ctx", "head"),
        P("ctx", "head"),
        P("ctx", "head"),
        P("ctx", "head"),
        P(),
        P(),
        P(),
        P("ctx"),
        P("ctx"),
        P(None, "head"),
    )
    return jax.shard_map(
        functools.partial(local, mesh),
        mesh=mesh,
        in_specs=placed,
        out_specs=(P("ctx", "head"), P("ctx", "head"), P("ctx", "head")),
        check_vma=False,
    )
```

```python
import functools

import jax
import jax.numpy as jnp
from jax import lax
from jax.experimental import pallas as pl
from jax.experimental.pallas import tpu as pltpu
from jax.sharding import PartitionSpec as P

HD = 128
BLOCK = 128
HOPS = 10
NBUCKET = 16
PAIR = 2
BACK = HOPS // PAIR
NCH = BACK + 1
KEYS = PAIR * BLOCK
KVROWS = 2 * BLOCK + 8
EPS = 1e-06
MESH = pl.DeviceIdType.MESH
F32 = jnp.float32
BF16 = jnp.bfloat16
EXP2_SCALE = (HD**-0.5) * 1.4426950408889634


def dot(a, b):
    return jnp.dot(a, b, preferred_element_type=F32)


def dot_nt(a, b):
    return lax.dot_general(a, b, (((1,), (1,)), ((), ())), preferred_element_type=F32)


def dot_t(a, b):
    return lax.dot_general(a, b, (((0,), (0,)), ((), ())), preferred_element_type=F32)


def kernel(
    n_ctx,
    n_head,
    heads,
    bucket_hbm,
    table_hbm,
    doc_hbm,
    qgain_hbm,
    kgain_hbm,
    q_hbm,
    k_hbm,
    v_hbm,
    g_hbm,
    w_hbm,
    gi_ref,
    gk_ref,
    gv_ref,
    bucket_ref,
    table_ref,
    doc_ref,
    qgain_ref,
    kgain_ref,
    q_ref,
    k_ref,
    v_ref,
    g_ref,
    w_ref,
    kvb,
    mask,
    qt,
    rq,
    qhat_t,
    g_t,
    gs_t,
    rows_of,
    total,
    out_t,
    expo,
    prods,
    ds,
    dq_t,
    dqr_t,
    part_tmp,
    part_own,
    part_out,
    part_in,
    comb,
    arrived,
    term_out,
    relay_in,
    term_in,
    own,
    in_sem,
    kv_send,
    kv_recv,
    fw_send,
    fw_recv,
    pt_send,
    pt_recv,
    cb_send,
    cb_recv,
    rs_send,
    rs_recv,
):
    me = lax.axis_index("ctx")
    hx = lax.axis_index("head")
    core = lax.rem(me, PAIR)
    sib = me + 1 - 2 * core
    other = 1 - core
    width = gi_ref.shape[1]
    quarter = width // 4
    pairs = heads // 2

    chip = lax.div(me, PAIR)
    chips = n_ctx // PAIR

    def has_back(step):
        return chip >= step

    def has_next(step):
        return chip + step < chips

    def ctx_at(step):
        return me + step * PAIR

    def head_at(step):
        return lax.rem(hx + step + n_head, n_head)

    barrier = pltpu.get_barrier_semaphore()

    def greet(target):
        pl.semaphore_signal(barrier, inc=1, device_id=target, device_id_type=MESH)

    for peer in [(sib, hx), (me, head_at(1)), (me, head_at(-1))]:
        greet(peer)
    for step in range(1, BACK + 1):

        @pl.when(has_back(step))
        def _():
            greet((ctx_at(-step), hx))

    loads = [
        pltpu.make_async_copy(src, dst, in_sem.at[i])
        for i, (src, dst) in enumerate(
            (
                (k_hbm, k_ref),
                (v_hbm, v_ref),
                (kgain_hbm, kgain_ref),
                (doc_hbm, doc_ref),
                (q_hbm, q_ref),
                (qgain_hbm, qgain_ref),
                (table_hbm, table_ref),
                (bucket_hbm, bucket_ref),
                (g_hbm, g_ref),
                (w_hbm, w_ref),
            )
        )
    ]
    for copy in loads:
        copy.start()

    for copy in loads[:4]:
        copy.wait()
    own_doc = jnp.full((1, HD), doc_ref[0], jnp.int32).astype(F32)
    k_f = k_ref[...].astype(F32)
    k_r = lax.rsqrt(jnp.mean(k_f * k_f, axis=-1, keepdims=True) + EPS)
    kvb[0, core, 0:BLOCK, :] = (k_f * k_r * kgain_ref[...]).astype(BF16)
    kvb[0, core, BLOCK : 2 * BLOCK, :] = v_ref[...]
    kvb[0, core, 2 * BLOCK : KVROWS, :] = jnp.broadcast_to(own_doc, (8, HD)).astype(BF16)
    pl.semaphore_wait(barrier, 3 + jnp.minimum(chips - 1 - chip, BACK))

    sends = []

    def remote(src, dst, send_sem, recv_sem, target):
        return pltpu.make_async_remote_copy(
            src_ref=src,
            dst_ref=dst,
            send_sem=send_sem,
            recv_sem=recv_sem,
            device_id=target,
            device_id_type=MESH,
        )

    def send(src, dst, send_sem, recv_sem, target):
        copy = remote(src, dst, send_sem, recv_sem, target)
        copy.start()
        sends.append((copy, None))
        return copy

    def send_if(cond, src, dst, send_sem, recv_sem, target):
        copy = remote(src, dst, send_sem, recv_sem, target)
        pl.when(cond)(copy.start)
        sends.append((copy, cond))
        return copy

    own_kv = kvb.at[0, core]
    fw = [send(own_kv, own_kv, fw_send.at[0], fw_recv.at[0], (sib, hx))]
    for j in range(1, NCH):
        slot = kvb.at[j, core]
        fw.append(remote(slot, slot, fw_send.at[j], fw_recv.at[j], (sib, hx)))
        sends.append((fw[j], has_back(j)))
    kv = [None]
    for j in range(1, NCH):
        kv.append(
            send_if(has_next(j), own_kv, kvb.at[j, core], kv_send.at[j], kv_recv.at[j], (ctx_at(j), hx))
        )

    for copy in loads[4:8]:
        copy.wait()
    weight = jnp.zeros((1, BLOCK), F32)
    for b in range(NBUCKET):
        weight = jnp.where(bucket_ref[...] == b, table_ref[b], weight)
    gain_t = jnp.broadcast_to(qgain_ref[...], (HD, HD)).T
    for h in range(heads):
        cols = pl.ds(h * HD, HD)
        x_t = q_ref[:, cols].T
        qt[cols, :] = x_t
        x = x_t.astype(F32)
        r = lax.rsqrt(jnp.mean(x * x, axis=0, keepdims=True) + EPS)
        rq[h : h + 1, :] = r
        qhat_t[:, cols] = (x * r * gain_t).astype(BF16)
    loads[8].wait()
    for h in range(heads):
        cols = pl.ds(h * HD, HD)
        g_t[:, cols] = g_ref[:, cols].T

    key_pos = lax.broadcasted_iota(jnp.int32, (KEYS, BLOCK), 0)
    row_pos = lax.broadcasted_iota(jnp.int32, (KEYS, BLOCK), 1) + core * BLOCK
    causal = jnp.where(key_pos <= row_pos, 1.0, 0.0)

    def both(j, first):
        return jnp.concatenate([kvb[j, b, first : first + BLOCK, :] for b in range(PAIR)], axis=0)

    def fetch(j):
        @pl.when(has_back(j))
        def _():
            kv[j].wait_recv()
            fw[j].start()

    def first_pass(j):
        fw[j].wait_recv()
        for b in range(PAIR):
            docs = kvb[j, b, 2 * BLOCK : KVROWS, :].astype(F32)[0:1]
            same = jnp.where(docs == own_doc, 1.0, 0.0)
            rows = slice(b * BLOCK, (b + 1) * BLOCK)
            if j == 0:
                mask[rows, :] = causal[rows] * same
            else:
                mask[rows, :] = jnp.broadcast_to(same, (BLOCK, BLOCK))
        keys, vals = both(j, 0), both(j, BLOCK)
        for p in range(pairs):
            cols = pl.ds(p * KEYS, KEYS)
            s = dot(keys, qhat_t[:, cols])
            m = mask[...]
            e = jnp.exp2(s * EXP2_SCALE) * jnp.concatenate([m, m], axis=1)
            part = jnp.sum(e.reshape(KEYS // 8, 8, KEYS), axis=0)
            e_half = e.astype(BF16)
            expo[j, :, cols] = e_half
            prods[j, :, cols] = dot(vals, g_t[:, cols])
            weighted = dot_t(vals, e_half)
            if j == 0:
                total[:, cols] = part
                out_t[:, cols] = weighted
            else:
                total[:, cols] += part
                out_t[:, cols] += weighted
            if p == 1 and j + 1 < NCH:
                fetch(j + 1)

    for j in range(NCH):
        if j == 0:
            first_pass(0)
        else:
            pl.when(has_back(j))(functools.partial(first_pass, j))

    for p in range(pairs):
        cols = pl.ds(p * KEYS, KEYS)
        inv = 1.0 / jnp.sum(total[:, cols], axis=0, keepdims=True)
        ratio = jnp.concatenate([weight, weight], axis=1) * inv
        g = g_t[:, cols].astype(F32)
        gs_t[:, cols] = (g * ratio).astype(BF16)
        rows_of[0:1, cols] = ratio
        rows_of[1:2, cols] = jnp.sum(g * out_t[:, cols], axis=0, keepdims=True) * (inv * ratio)

    def second_pass(j):
        keys = both(j, 0)
        for p in range(pairs):
            cols = pl.ds(p * KEYS, KEYS)
            e = expo[j, :, cols].astype(F32)
            d = (e * (prods[j, :, cols] * rows_of[0:1, cols] - rows_of[1:2, cols])).astype(BF16)
            ds[j, :, cols] = d
            dq = dot_t(keys, d)
            if j == 0:
                dq_t[:, cols] = dq
            else:
                dq_t[:, cols] += dq

    for j in range(NCH):
        if j == 0:
            second_pass(0)
        else:
            pl.when(has_back(j))(functools.partial(second_pass, j))

    for h in range(heads):
        cols = pl.ds(h * HD, HD)
        r = rq[h : h + 1, :]
        xn = qt[cols, :].astype(F32) * r
        gc = gain_t * (dq_t[:, cols] * (HD**-0.5))
        back = r * (gc - xn * jnp.mean(xn * gc, axis=0, keepdims=True))
        dqr_t[cols, :] = back.astype(BF16)

    loads[9].wait()

    def term(step, part):
        first = pl.multiple_of(head_at(step) * width + part * quarter, quarter)
        return dot(w_ref[pl.ds(first, quarter), :], dqr_t[...])

    def hand(slot, value, dst, step):
        term_out[slot] = value.astype(BF16)
        return send(term_out.at[slot], dst, rs_send.at[slot], rs_recv.at[slot], (me, head_at(step)))

    def relay(side, q):
        part = term(2, q + 2 * side)
        return hand(side * 6 + q, part, relay_in.at[side, q], 1 - 2 * side)

    def direct(side, q):
        at = q + 2 - 2 * side
        part = term(1 - 2 * side, at)
        return hand(side * 6 + 2 + q, part, term_in.at[side, at], 1 - 2 * side)

    def summed(side, q, arriving):
        at = q + 2 * side
        part = term(1 - 2 * side, at)
        arriving.wait_recv()
        part = part + relay_in[side, q].astype(F32)
        return hand(side * 6 + 4 + q, part, term_in.at[side, at], 1 - 2 * side)

    mine = pl.ds(pl.multiple_of(core * BLOCK, BLOCK), BLOCK)
    theirs = pl.ds(pl.multiple_of(other * BLOCK, BLOCK), BLOCK)
    pt = [
        remote(part_out.at[j], part_in.at[j], pt_send.at[j], pt_recv.at[j], (sib, hx)) for j in range(NCH)
    ]
    cb = [None] + [
        remote(comb.at[j], arrived.at[j], cb_send.at[j], cb_recv.at[j], (ctx_at(-j), hx))
        for j in range(1, NCH)
    ]
    for j in range(NCH):
        always = None if j == 0 else has_back(j)
        sends.append((pt[j], always))
        if j > 0:
            sends.append((cb[j], always))

    def share(j):
        part_tmp[0] = dot_nt(qhat_t[...], ds[j])
        part_tmp[1] = dot_nt(gs_t[...], expo[j])
        for i in range(2):
            rows = slice(i * BLOCK, (i + 1) * BLOCK)
            part_own[j, rows, :] = part_tmp[i, :, mine]
            part_out[j, rows, :] = part_tmp[i, :, theirs].astype(BF16)
        pt[j].start()

    def pass_on(j):
        pt[j].wait_recv()
        summed = part_own[j] + part_in[j].astype(F32)
        if j > 0:
            comb[j] = summed.astype(BF16)
            cb[j].start()
        else:
            part_own[0] = summed

    def shares(chunks):
        for j in chunks:
            pl.when(has_back(j))(functools.partial(share, j))
            if j + 1 < NCH:
                pl.when(has_back(j + 1))(functools.partial(pass_on, j + 1))

    relayed = {(side, q): relay(side, q) for q in range(2) for side in range(2)}
    shares((5, 4))
    straight = {(side, q): direct(side, q) for q in range(2) for side in range(2)}
    shares((3, 2, 1))
    added = {(side, 0): summed(side, 0, relayed[side, 0]) for side in range(2)}
    pl.when(has_back(1))(functools.partial(pass_on, 1))
    added |= {(side, 1): summed(side, 1, relayed[side, 1]) for side in range(2)}
    share(0)
    for q in range(4):
        own[q] = term(0, q)

    pass_on(0)
    for j in range(NCH - 1, 0, -1):

        @pl.when(has_next(j))
        def _():
            cb[j].wait_recv()
            part_own[0] += arrived[j].astype(F32)

    gv_ref[...] = part_own[0, BLOCK:, :].T.astype(BF16)
    k_f = k_ref[...].astype(F32)
    k_r = lax.rsqrt(jnp.mean(k_f * k_f, axis=-1, keepdims=True) + EPS)
    xn = k_f * k_r
    gc = kgain_ref[...] * (part_own[0, :BLOCK, :].T * (HD**-0.5))
    gk_ref[...] = (k_r * (gc - xn * jnp.mean(xn * gc, axis=-1, keepdims=True))).astype(BF16)

    for q, arrivals in (
        (0, (added[0, 0], straight[1, 0])),
        (2, (straight[0, 0], added[1, 0])),
        (1, (added[0, 1], straight[1, 1])),
        (3, (straight[0, 1], added[1, 1])),
    ):
        for copy in arrivals:
            copy.wait_recv()
        sum_t = (own[q] + term_in[0, q].astype(F32) + term_in[1, q].astype(F32)).astype(BF16)
        for b in range(quarter // BLOCK):
            first = q * quarter + b * BLOCK
            gi_ref[:, first : first + BLOCK] = sum_t[b * BLOCK : (b + 1) * BLOCK].T

    for copy, cond in sends:
        if cond is None:
            copy.wait_send()
        else:
            pl.when(cond)(copy.wait_send)


def hand_out(a, b, c, a_out, b_out, c_out, sem):
    copies = [
        pltpu.make_async_copy(src, dst, sem.at[i])
        for i, (src, dst) in enumerate(((a, a_out), (b, b_out), (c, c_out)))
    ]
    for copy in copies:
        copy.start()
    for copy in copies:
        copy.wait()


def local(mesh, *args):
    q, k, v, g, q_gain, k_gain, table, bucket, docs, w = args
    n_ctx, n_head = mesh.shape["ctx"], mesh.shape["head"]
    tokens, features = q.shape
    heads = features // HD
    cols = heads * BLOCK
    width = w.shape[0] // n_head
    quarter = width // 4
    vmem = pl.BlockSpec(memory_space=pltpu.VMEM)
    smem = pl.BlockSpec(memory_space=pltpu.SMEM)
    hbm = pl.BlockSpec(memory_space=pl.ANY)
    dma = pltpu.SemaphoreType.DMA
    results = pl.pallas_call(
        functools.partial(kernel, n_ctx, n_head, heads),
        out_shape=(
            pltpu.VMEM((tokens, width), BF16),
            pltpu.VMEM(k.shape, BF16),
            pltpu.VMEM(v.shape, BF16),
        ),
        in_specs=[hbm, pl.BlockSpec(memory_space=pltpu.HBM), pl.BlockSpec(memory_space=pltpu.HBM)] + [hbm] * 7,
        out_specs=(vmem, vmem, vmem),
        scratch_shapes=[
            pltpu.VMEM((1, tokens), jnp.int32),
            pltpu.SMEM((NBUCKET,), F32),
            pltpu.SMEM((1,), jnp.int32),
            pltpu.VMEM((1, HD), F32),
            pltpu.VMEM((1, HD), F32),
            pltpu.VMEM(q.shape, BF16),
            pltpu.VMEM(k.shape, BF16),
            pltpu.VMEM(v.shape, BF16),
            pltpu.VMEM(g.shape, BF16),
            pltpu.VMEM(w.shape, BF16),
            pltpu.VMEM((NCH, PAIR, KVROWS, HD), BF16),
            pltpu.VMEM((KEYS, BLOCK), F32),
            pltpu.VMEM((cols, BLOCK), BF16),
            pltpu.VMEM((heads, BLOCK), F32),
            pltpu.VMEM((HD, cols), BF16),
            pltpu.VMEM((HD, cols), BF16),
            pltpu.VMEM((HD, cols), BF16),
            pltpu.VMEM((8, cols), F32),
            pltpu.VMEM((8, cols), F32),
            pltpu.VMEM((HD, cols), F32),
            pltpu.VMEM((NCH, KEYS, cols), BF16),
            pltpu.VMEM((NCH, KEYS, cols), F32),
            pltpu.VMEM((NCH, KEYS, cols), BF16),
            pltpu.VMEM((HD, cols), F32),
            pltpu.VMEM((cols, BLOCK), BF16),
            pltpu.VMEM((2, HD, KEYS), F32),
            pltpu.VMEM((NCH, 2 * BLOCK, HD), F32),
            pltpu.VMEM((NCH, 2 * BLOCK, HD), BF16),
            pltpu.VMEM((NCH, 2 * BLOCK, HD), BF16),
            pltpu.VMEM((NCH, 2 * BLOCK, HD), BF16),
            pltpu.VMEM((NCH, 2 * BLOCK, HD), BF16),
            pltpu.VMEM((12, quarter, BLOCK), BF16),
            pltpu.VMEM((2, 2, quarter, BLOCK), BF16),
            pltpu.VMEM((2, 4, quarter, BLOCK), BF16),
            pltpu.VMEM((4, quarter, BLOCK), F32),
            dma((10,)),
            dma((NCH,)),
            dma((NCH,)),
            dma((NCH,)),
            dma((NCH,)),
            dma((NCH,)),
            dma((NCH,)),
            dma((NCH,)),
            dma((NCH,)),
            dma((12,)),
            dma((12,)),
        ],
        compiler_params=pltpu.CompilerParams(
            collective_id=0, has_side_effects=True, vmem_limit_bytes=56 * 1024 * 1024
        ),
    )(bucket.reshape(1, tokens), table, docs, q_gain.reshape(1, HD), k_gain.reshape(1, HD), q, k, v, g, w)
    return pl.pallas_call(
        hand_out,
        out_shape=tuple(jax.ShapeDtypeStruct(r.shape, r.dtype) for r in results),
        in_specs=[vmem] * 3,
        out_specs=(hbm,) * 3,
        scratch_shapes=[dma((3,))],
    )(*(pltpu.with_memory_space_constraint(r, pltpu.VMEM) for r in results))


def solution(mesh):
    placed = (
        P("ctx", "head"),
        P("ctx", "head"),
        P("ctx", "head"),
        P("ctx", "head"),
        P(),
        P(),
        P(),
        P("ctx"),
        P("ctx"),
        P(None, "head"),
    )
    return jax.shard_map(
        functools.partial(local, mesh),
        mesh=mesh,
        in_specs=placed,
        out_specs=(P("ctx", "head"), P("ctx", "head"), P("ctx", "head")),
        check_vma=False,
    )
```
